32 devices in a mesh: groups: 2 (over x), ctx: 8 (over z, y), head: 2 (over core).
Axes of the slice: x: 2, y: 2, z: 4, core: 2. Of those that a mesh axis runs over, the one named last changes fastest.
Arguments:
- query_nope: bfloat16 [32, 128, 128], P('groups', ('ctx', 'head')), parts along dimension 0, may hold values from -6 to 6
- query_rope: bfloat16 [32, 8192], P('groups', ('ctx', 'head')), parts along dimension 0, may hold values from -31 to 31
- key_absorb: bfloat16 [128, 128, 512], P(('ctx', 'head')), may hold values from -0.5 to 0.5
- value_absorb: bfloat16 [128, 512, 128], P(('ctx', 'head')), may hold values from -4 to 4
- output_weight: bfloat16 [16384, 7168], P(('ctx', 'head')), may hold values from -0.0625 to 0.0625
- latent_cache: bfloat16 [3584, 64, 576], P(('groups', 'ctx')), parts along dimension 0, may hold values from -4 to 4
- page_owner: int32 [3584], P(('groups', 'ctx')), parts along dimension 0, may hold values from -1 to 15, as said below
Outputs:
- layer_output: bfloat16 [32, 7168], P('groups', ('ctx', 'head')), parts along dimension 0
The draws below stay inside these ranges and needn't reach their ends.
There are 2 independent parts, one for each index of `groups`. The reference program is written for one: setup_inputs(seed, part) draws one part's arguments, and reference() takes and returns one part's arrays. A program takes and returns all parts, laid end to end along the dimension named above; an argument that names none is the same for every part. Nothing has to cross between parts.
Inputs may be any that keep to these rules, and one draw needn't show every extreme that they name: `page_owner`: a slot's request, or -1 for an unused slot; every request owns at least one slot; every index of ctx has an eighth of its 224 slots or more in use, and some index has all 224 in use.
All inputs are finite; a program needn't handle non-finite values.
Results may differ from the reference program's by a relative error of at most 0.03.
Values may be sent and summed in bfloat16 or wider, within the bound.
A program may use at most 128 MiB of HBM per device.

```python
import jax
import jax.numpy as jnp
from jax import lax

D = 7168
H = 128
DN = 128
DR = 64
LAT = 512
DV = 128
PAGE = 64
BLOCK_PAGES = 8
R = 16
PAGES_DEV = 224
POOL = 1792
KV = 576


def load_pattern():
    device_count = POOL // PAGES_DEV
    lowest = PAGES_DEV // 8
    spread = max(device_count - 1, 1)
    return [lowest + (PAGES_DEV - lowest) * device * device // (spread * spread) for device in range(device_count)]


def page_layout(key):
    pattern = load_pattern()
    filled = sum(pattern)
    device_count = len(pattern)
    shuffled = jax.random.permutation(jax.random.fold_in(key, 11), device_count)
    device_load = jnp.array(pattern, jnp.int32)[shuffled]
    slot_ids = jnp.arange(POOL, dtype=jnp.int32)
    in_use = slot_ids % PAGES_DEV < device_load[slot_ids // PAGES_DEV]
    ranked = jnp.clip(jnp.cumsum(in_use.astype(jnp.int32)) - 1, 0, filled - 1)
    logical = jax.random.permutation(jax.random.fold_in(key, 13), filled).astype(jnp.int32)[ranked]
    boundary = jnp.sort(jax.random.permutation(jax.random.fold_in(key, 12), filled - 1).astype(jnp.int32)[:R - 1] + 1)
    owners = jnp.sum((logical[:, None] >= boundary[None, :]).astype(jnp.int32), axis=1)
    return jnp.where(in_use, owners, -1).astype(jnp.int32)


def draw_page_owner(key, part):
    owners = page_layout(key)
    return owners


def draw_latent_cache(key, part):
    latent = jax.random.truncated_normal(jax.random.fold_in(key, 21), -4.0, 4.0, (POOL, PAGE, LAT), jnp.float32)
    rope_part = jax.random.truncated_normal(jax.random.fold_in(key, 22), -4.0, 4.0, (POOL, PAGE, DR), jnp.float32)
    return jnp.concatenate([latent, rope_part], axis=2).astype(jnp.bfloat16)


def draw_query_rope(key, part):
    values = jax.random.truncated_normal(jax.random.fold_in(key, 32), -4.0, 4.0, (R, H, DR), jnp.float32)
    return values.reshape(R, H * DR).astype(jnp.bfloat16)


def strengthened(drawn, key, source, target, shards_of, factor):
    owner, partner = [(jnp.arange(drawn.shape[dim]) // (drawn.shape[dim] // shards_of)).reshape([-1 if axis == dim else 1 for axis in range(drawn.ndim)]) for dim in (source, target)]
    chosen = jax.random.permutation(key, shards_of)[partner]
    strong = (owner == chosen) | (owner == (partner + shards_of // 2) % shards_of)
    return jnp.where(strong, factor * drawn, drawn)


def block_scale(own_key, shape, cuts, low, high):
    factor_of, own = 1.0, jax.random.fold_in(own_key, 6)
    for dim, blocks in cuts:
        heights = jnp.exp(jax.random.uniform(jax.random.fold_in(own, dim), (blocks,), jnp.float32, low / len(cuts), high / len(cuts)))
        factor_of = factor_of * jnp.repeat(heights, shape[dim] // blocks).reshape([-1 if axis == dim else 1 for axis in range(len(shape))])
    return factor_of


def normal_values(own_key, extent, scale, bound, split=(), kind=jnp.bfloat16):
    values = jax.random.normal(own_key, extent, jnp.float32) * scale
    if len(split) > 0:
        values = block_scale(own_key, extent, split, -0.22, 0.18) * values
    return jnp.clip(values, min=-bound, max=bound).astype(kind)


def noise_with(rng, dims, scale, limit, cuts, heavy, held_as=jnp.bfloat16):
    values = scale * jax.random.normal(rng, dims, jnp.float32)
    if cuts:
        values = values * block_scale(rng, dims, cuts, -0.22, 0.18)
    return jnp.clip(strengthened(values, jax.random.fold_in(rng, 3), *heavy), -limit, limit).astype(held_as)


def setup_inputs(seed: int = 0, part: int = 0) -> dict:
    keys = jax.random.split(jax.random.key(seed), 8)
    own_keys = jax.random.split(jax.random.fold_in(keys[7], part), 8)
    query_nope = normal_values(own_keys[0], (R, H, DN), 1.0, 6.0, ((1, 16),))
    query_rope = draw_query_rope(jax.random.fold_in(jax.random.fold_in(keys[7], part), 71), part)
    key_absorb = normal_values(keys[2], (H, DN, LAT), DN ** -0.5, 0.5, ((0, 16),))
    value_absorb = normal_values(keys[3], (H, LAT, DV), 0.7, 4.0, ((0, 16),))
    output_weight = noise_with(keys[4], (H * DV, D), (H * DV) ** -0.5, 0.0625, ((0, 16),), (0, 1, 16, 2.0))
    latent_cache = draw_latent_cache(jax.random.fold_in(jax.random.fold_in(keys[7], part), 71), part)
    page_owner = draw_page_owner(jax.random.fold_in(jax.random.fold_in(keys[7], part), 71), part)
    return {"query_nope": query_nope, "query_rope": query_rope, "key_absorb": key_absorb, "value_absorb": value_absorb, "output_weight": output_weight, "latent_cache": latent_cache, "page_owner": page_owner}


masked_score = -1.0e30
highest = lax.Precision.HIGHEST


def reference(query_nope, query_rope, key_absorb, value_absorb, output_weight, latent_cache, page_owner):
    score_scale = (DN + DR) ** -0.5
    query_latent = jnp.einsum("rhn,hnl->rhl", query_nope.astype(jnp.float32), key_absorb.astype(jnp.float32), precision=highest).astype(jnp.bfloat16)
    query_full = jnp.concatenate([query_latent, query_rope.reshape(R, H, DR)], axis=2)
    block_count = POOL // BLOCK_PAGES
    cache_blocks = latent_cache.reshape(block_count, BLOCK_PAGES, PAGE, KV)
    owner_blocks = page_owner.reshape(block_count, BLOCK_PAGES)

    def score_block(inputs):
        page_rows, owner_ids = inputs
        page_query = query_full[jnp.clip(owner_ids, 0, R - 1)]
        scores = jnp.einsum("ptk,phk->pth", page_rows.astype(jnp.float32), page_query.astype(jnp.float32), precision=highest) * score_scale
        return jnp.where((owner_ids >= 0)[:, None, None], scores, masked_score)

    block_scores = lax.map(score_block, (cache_blocks, owner_blocks))
    page_max = jnp.max(block_scores, axis=2).reshape(POOL, H)
    owner_hot = page_owner[:, None] == jnp.arange(R, dtype=jnp.int32)[None, :]
    row_max = jnp.max(jnp.where(owner_hot[:, :, None], page_max[:, None, :], masked_score), axis=0)

    def sum_block(state, inputs):
        running_sum, running_total = state
        page_rows, owner_ids, scores = inputs
        onehot = (owner_ids[:, None] == jnp.arange(R, dtype=jnp.int32)[None, :]).astype(jnp.float32)
        offset = row_max[jnp.clip(owner_ids, 0, R - 1)]
        weights = jnp.where((owner_ids >= 0)[:, None, None], jnp.exp(scores - offset[:, None, :]), 0.0)
        weight_half = weights.astype(jnp.bfloat16).astype(jnp.float32)
        page_out = jnp.einsum("pth,ptl->phl", weight_half, page_rows[:, :, :LAT].astype(jnp.float32), precision=highest)
        running_sum = running_sum + jnp.einsum("pr,phl->rhl", onehot, page_out, precision=highest)
        running_total = running_total + jnp.einsum("pr,ph->rh", onehot, jnp.sum(weights, axis=1), precision=highest)
        return (running_sum, running_total), None

    start_state = (jnp.zeros((R, H, LAT), jnp.float32), jnp.zeros((R, H), jnp.float32))
    (latent_sum, total), _ = lax.scan(sum_block, start_state, (cache_blocks, owner_blocks, block_scores))
    attended = (latent_sum / total[:, :, None]).astype(jnp.bfloat16)
    head_out = jnp.einsum("rhl,hlv->rhv", attended.astype(jnp.float32), value_absorb.astype(jnp.float32), precision=highest).astype(jnp.bfloat16)
    return jnp.dot(head_out.reshape(R, H * DV), output_weight, preferred_element_type=jnp.float32).astype(jnp.bfloat16)
```

```python
import functools

import jax
import jax.numpy as jnp
from jax import lax
from jax.experimental import pallas as pl
from jax.experimental.pallas import tpu as pltpu
from jax.sharding import PartitionSpec as P

PARTS = 2
GROUP = 4
F32 = jnp.float32
BF16 = jnp.bfloat16
I32 = jnp.int32
LOW = -1e30


def dot_nt(a, b):
    return lax.dot_general(a, b, (((1,), (1,)), ((), ())), preferred_element_type=F32)


def remote(src, dst, send_sem, recv_sem, where):
    return pltpu.make_async_remote_copy(
        src_ref=src, dst_ref=dst, send_sem=send_sem, recv_sem=recv_sem,
        device_id=where, device_id_type=pl.DeviceIdType.MESH)


def up_to(n, step):
    return -(-n // step) * step


def column(row):
    n = row.shape[1]
    diagonal = lax.broadcasted_iota(I32, (n, n), 0) == lax.broadcasted_iota(I32, (n, n), 1)
    return jnp.sum(jnp.where(diagonal, jnp.broadcast_to(row, (n, n)), 0), axis=1, keepdims=True)


def plan_items(owner, requests, group, table, bias):
    count = owner.shape[1]
    width = up_to(count, 128)
    lanes_out = table.shape[1]
    items, tokens = bias.shape
    page = tokens // group
    owner = jnp.where(owner < 0, requests, owner)
    if width > count:
        owner = jnp.concatenate([owner, jnp.full((1, width - count), requests, I32)], axis=1)
    lane = lax.broadcasted_iota(I32, (1, width), 1)
    slot = lax.broadcasted_iota(I32, (width, 1), 0)
    lanes = lax.broadcasted_iota(I32, (width, width), 1)
    places = lax.broadcasted_iota(I32, (width, width), 0)
    key = owner * width + lane
    rank = jnp.sum(jnp.where(jnp.broadcast_to(key, (width, width)) < column(key), 1, 0), axis=1, keepdims=True)
    owner_c = column(owner)
    here = rank == lanes
    order = jnp.sum(jnp.where(here, slot, 0), axis=0, keepdims=True)
    sorted_owner = jnp.sum(jnp.where(here, owner_c, 0), axis=0, keepdims=True)
    before = jnp.sum(jnp.where(rank + 1 == lanes, owner_c, 0), axis=0, keepdims=True)
    opens = (lax.rem(lane, jnp.full(lane.shape, group, I32)) == 0) | (sorted_owner != before)
    start = column(jnp.where(opens & (sorted_owner < requests), 1, 0))
    order_c, sorted_c = column(order), column(sorted_owner)
    item = column(jnp.sum(jnp.where(places <= lanes, start, 0), axis=0, keepdims=True) - 1)
    place = lax.broadcasted_iota(I32, (width, lanes_out), 0)
    mine = (item == lax.broadcasted_iota(I32, (width, lanes_out), 1)) & (start > 0)

    def pick(value):
        return jnp.sum(jnp.where(mine, value, 0), axis=0, keepdims=True)

    first, who, real = pick(slot), pick(sorted_c), pick(start)
    first = first - lax.rem(first, jnp.full(first.shape, group, I32))
    tag = jnp.where(real > 0, who, -1)
    tag_c = column(tag)
    table[0:1, :] = who
    for j in range(group):
        chosen = place == first + j
        table[1 + j:2 + j, :] = jnp.sum(jnp.where(chosen, order_c, 0), axis=0, keepdims=True)
        theirs = column(jnp.sum(jnp.where(chosen, sorted_c, 0), axis=0, keepdims=True))
        fits = jnp.where(theirs[:items] == tag_c[:items], 0.0, LOW)
        bias[:, j * page:(j + 1) * page] = jnp.broadcast_to(fits, (items, page))
    index = lax.broadcasted_iota(I32, (1, lanes_out), 1)
    previous = jnp.where(index == 0, -1, pltpu.roll(tag, 1, 1))
    table[group + 1:group + 2, :] = jnp.where(tag == previous, 1, 0)
    owned = tag_c == lax.broadcasted_iota(I32, (lanes_out, lanes_out), 1)
    number = lax.broadcasted_iota(I32, (lanes_out, lanes_out), 0)
    table[group + 2:group + 3, :] = jnp.max(jnp.where(owned, number, 0), axis=0, keepdims=True)
    table[group + 3:group + 4, :] = jnp.max(jnp.where(owned, 1, 0), axis=0, keepdims=True)


def kernel(ctx, unroll, score_scale, nope_hbm, rope_hbm, key_hbm, owner_hbm, cache_hbm, value_hbm, weight_hbm, out_ref,
           nope_ref, rope_ref, key_ref, value_ref, weight, pages, in_sems, wide, rows_a, rows_b, mine_a, mine_b,
           all_a, all_b, y_send, y_recv, up_send, up_recv, down_send, down_recv,
           owner_ref, table, tab, bias, query_a, query_b, scores, marks, top_full, acc,
           sums, stats, y_sum, y_stat, c_sum, c_stat, z_sum, z_stat, attended,
           h_keep, h_out, h_in, p_out, p_in,
           ys_send, ys_recv, yt_send, yt_recv, zs_send, zs_recv, zt_send, zt_recv,
           h_send, h_recv, p_send, p_recv):
    requests, heads_here, _ = nope_ref.shape
    latent = key_ref.shape[2]
    cut = query_b.shape[2]
    rope = rope_ref.shape[1] // heads_here
    items = scores.shape[0]
    nz = ctx // 2
    half = out_ref.shape[1]
    block = 2 * half
    me, core = lax.axis_index("ctx"), lax.axis_index("head")
    z, y = me // 2, me % 2
    partner, twin = {"ctx": z * 2 + 1 - y}, {"head": 1 - core}
    above, below = {"ctx": me + 2}, {"ctx": me - 2}
    has_above, has_below = z + 1 < nz, z > 0

    def load(i, src, dst):
        return pltpu.make_async_copy(src, dst, in_sems.at[i])

    first_loads = [load(0, nope_hbm, nope_ref), load(1, rope_hbm, rope_ref), load(2, key_hbm, key_ref)]
    owner_load = load(3, owner_hbm, owner_ref)
    cache_load, value_load, weight_load = (
        load(4, cache_hbm, pages), load(5, value_hbm, value_ref), load(6, weight_hbm, weight))
    table_load = load(7, table, tab)
    for copy in first_loads:
        copy.start()
    owner_load.start()

    barrier = pltpu.get_barrier_semaphore()
    for k in range(1, ctx):
        pl.semaphore_signal(barrier, inc=1, device_id={"ctx": (me + k) % ctx}, device_id_type=pl.DeviceIdType.MESH)
    pl.semaphore_signal(barrier, inc=1, device_id=twin, device_id_type=pl.DeviceIdType.MESH)

    for copy in first_loads:
        copy.wait()
    cache_load.start()
    wide[...] = nope_ref[...].astype(F32)
    depth = mine_a.shape[0] // PARTS
    gathered = (all_a, all_b)

    def lines(part):
        return slice(part * depth, (part + 1) * depth)

    def block_of(which, row, part):
        return gathered[which].at[row, lines(part)]

    def sem(which, step, part):
        return (which * nz + step) * PARTS + part

    def across(which, origin, part, src=None):
        slot, i = block_of(which, origin * 2 + y, part), sem(which, origin, part)
        return remote(slot if src is None else src.at[lines(part)], slot, y_send.at[i], y_recv.at[i], partner)

    def upward(which, step, part, src=None):
        slot, i = block_of(which, me - 2 * step, part), sem(which, step, part)
        return remote(slot if src is None else src.at[lines(part)], slot, up_send.at[i], up_recv.at[i], above)

    def downward(which, step, part, src=None):
        slot, i = block_of(which, me + 2 * step, part), sem(which, step, part)
        return remote(slot if src is None else src.at[lines(part)], slot, down_send.at[i], down_recv.at[i], below)

    def arrival(which, row, part, done):
        slot = block_of(which, row, part)
        return remote(slot, slot, done, done, partner)

    mine = (mine_a, mine_b)

    def send_own(which):
        for part in range(PARTS):
            @pl.when(has_above)
            def _():
                upward(which, 0, part, mine[which]).start()

            @pl.when(has_below)
            def _():
                downward(which, 0, part, mine[which]).start()

            across(which, z, part, mine[which]).start()

    for h in range(heads_here):
        flat = wide[:, h, :].astype(BF16)
        rows_a[:, h, :cut] = jnp.dot(flat, key_ref[h, :, :cut], preferred_element_type=F32)
        rows_a[:, h, cut:] = rope_ref[:, h * rope:(h + 1) * rope].astype(F32)
    value = rows_a[...].reshape(requests * heads_here, cut + rope).astype(BF16)
    mine_a[...] = value
    all_a[me] = value
    pl.semaphore_wait(barrier, ctx)
    send_own(0)
    for h in range(heads_here):
        rows_b[:, h, :] = jnp.dot(wide[:, h, :].astype(BF16), key_ref[h, :, cut:], preferred_element_type=F32)
    value = rows_b[...].reshape(requests * heads_here, latent - cut).astype(BF16)
    mine_b[...] = value
    all_b[me] = value
    send_own(1)
    value_load.start()
    weight_load.start()

    owner_load.wait()
    plan_items(owner_ref[...], requests, GROUP, table, bias)
    table_load.start()

    def pass_on(which, step):
        for part in range(PARTS):
            @pl.when(z - 1 - step >= 0)
            def _():
                arrival(which, me - 2 * (step + 1), part, up_recv.at[sem(which, step, part)]).wait_recv()
                if step + 1 < nz - 1:
                    @pl.when(has_above)
                    def _():
                        upward(which, step + 1, part).start()
                across(which, z - 1 - step, part).start()

            @pl.when(z + 1 + step < nz)
            def _():
                arrival(which, me + 2 * (step + 1), part, down_recv.at[sem(which, step, part)]).wait_recv()
                if step + 1 < nz - 1:
                    @pl.when(has_below)
                    def _():
                        downward(which, step + 1, part).start()
                across(which, z + 1 + step, part).start()

    for step in range(nz - 1):
        pass_on(0, step)
        if step >= 1:
            pass_on(1, step - 1)
    pass_on(1, nz - 2)

    def settle(which, query):
        for origin in range(nz):
            for part in range(PARTS):
                arrival(which, origin * 2 + 1 - y, part, y_recv.at[sem(which, origin, part)]).wait_recv()
        for r in range(requests):
            lots = [gathered[which][c, r * heads_here:(r + 1) * heads_here, :].astype(F32) for c in range(ctx)]
            query[r] = jnp.concatenate(lots, axis=0).astype(BF16)

    settle(0, query_a)
    table_load.wait()
    cache_load.wait()

    def entries(i, columns):
        return jnp.concatenate([pages[tab[1 + j, i], :, columns] for j in range(GROUP)], axis=0)

    def first_scores(s, carry):
        for u in range(unroll):
            i = s * unroll + u
            asked = query_a.at[tab[0, i]]
            scores[i] = (dot_nt(asked[:, :cut], entries(i, slice(0, cut)))
                         + dot_nt(asked[:, cut:], entries(i, slice(latent, latent + rope))))
        return carry

    lax.fori_loop(0, items // unroll, first_scores, 0)
    settle(1, query_b)

    def last_scores(s, top):
        for u in range(unroll):
            i = s * unroll + u
            found = scores[i] + dot_nt(query_b[tab[0, i]], entries(i, slice(cut, latent)))
            found = found * score_scale + bias[pl.ds(i, 1), :]
            scores[i] = found
            top = jnp.where(tab[GROUP + 1, i] > 0, top, LOW)
            for j in range(found.shape[1] // 128):
                top = jnp.maximum(top, found[:, j * 128:(j + 1) * 128])
            marks[i] = top
        return top

    lax.fori_loop(0, items // unroll, last_scores, jnp.full(marks.shape[1:], LOW, F32))
    for r in range(requests):
        seen = marks[tab[GROUP + 2, r]]
        top_full[r] = jnp.broadcast_to(jnp.max(seen, axis=1, keepdims=True), seen.shape)

    def weigh(s, carry):
        total, held = carry
        for u in range(unroll):
            i = s * unroll + u
            keep = tab[GROUP + 1, i] > 0
            top = top_full[tab[0, i]]
            total = jnp.where(keep, total, 0.0)
            weights = []
            for j in range(scores.shape[2] // 128):
                weight_j = jnp.exp(scores[i, :, j * 128:(j + 1) * 128] - top)
                total = total + weight_j
                weights.append(weight_j.astype(BF16))
            marks[i] = total
            held = jnp.where(keep, held, 0.0) + jnp.dot(
                jnp.concatenate(weights, axis=1), entries(i, slice(0, latent)), preferred_element_type=F32)
            acc[i] = held
        return total, held

    lax.fori_loop(0, items // unroll, weigh, (jnp.zeros(marks.shape[1:], F32), jnp.zeros(acc.shape[1:], F32)))

    lane = lax.broadcasted_iota(I32, marks.shape[1:], 1)
    top = jnp.full(lane.shape, LOW, F32)
    norm = jnp.zeros(lane.shape, F32)
    for r in range(requests):
        here = (lane == r) & jnp.broadcast_to(tab[GROUP + 3, r] > 0, lane.shape)
        top = jnp.where(here, top_full[r], top)
        norm = jnp.where(here, jnp.sum(marks[tab[GROUP + 2, r]], axis=1, keepdims=True), norm)
    for c in range(ctx):
        rows = slice(c * heads_here, (c + 1) * heads_here)
        stats[c % 2, c // 2, 0] = top[rows]
        stats[c % 2, c // 2, 1] = norm[rows]
        lots = [acc[tab[GROUP + 2, r], rows, :] for r in range(requests)]
        sums[c % 2, c // 2] = jnp.concatenate(lots, axis=0).astype(BF16)

    stat_copy = remote(stats.at[1 - y], y_stat, yt_send, yt_recv, partner)
    stat_copy.start()
    y_copies = []
    for k in range(nz):
        target = (z + 1 + k) % nz
        for part in range(PARTS):
            i = k * PARTS + part
            copy = remote(sums.at[1 - y, target, lines(part)], y_sum.at[k, lines(part)],
                          ys_send.at[i], ys_recv.at[i], partner)
            copy.start()
            y_copies.append(copy)
    stat_copy.wait_recv()

    def spread(factor):
        return jnp.concatenate([factor[:, r:r + 1] for r in range(requests)], axis=0)

    z_copies, z_stats = [], []
    for k in range(nz):
        target = (z + 1 + k) % nz
        top_a, norm_a = stats[y, target, 0], stats[y, target, 1]
        top_b, norm_b = y_stat[target, 0], y_stat[target, 1]
        top = jnp.maximum(top_a, top_b)
        keep_a, keep_b = jnp.exp(top_a - top), jnp.exp(top_b - top)
        norm = keep_a * norm_a + keep_b * norm_b
        rows_x, rows_y = spread(keep_a), spread(keep_b)
        there = {"ctx": target * 2 + y}
        if k < nz - 1:
            c_stat[k, 0] = top
            c_stat[k, 1] = norm
            copy = remote(c_stat.at[k], z_stat.at[k], zt_send.at[k], zt_recv.at[k], there)
            copy.start()
            z_stats.append(copy)
        both = []
        for part in range(PARTS):
            i = k * PARTS + part
            y_copies[i].wait_recv()
            both.append(rows_x[lines(part)] * sums[y, target, lines(part)].astype(F32)
                        + rows_y[lines(part)] * y_sum[k, lines(part)].astype(F32))
            if k < nz - 1:
                c_sum[k, lines(part)] = both[part].astype(BF16)
                copy = remote(c_sum.at[k, lines(part)], z_sum.at[k, lines(part)], zs_send.at[i], zs_recv.at[i], there)
                copy.start()
                z_copies.append(copy)
    both = jnp.concatenate(both, axis=0)
    for copy in z_stats:
        copy.wait_recv()
    highest = top
    for k in range(nz - 1):
        highest = jnp.maximum(highest, z_stat[k, 0])
    keep = jnp.exp(top - highest)
    all_norm = keep * norm
    factors = []
    for k in range(nz - 1):
        factors.append(jnp.exp(z_stat[k, 0] - highest))
        all_norm = all_norm + factors[k] * z_stat[k, 1]
    safe = jnp.where(all_norm > 0, all_norm, 1.0)
    total = spread(keep / safe) * both
    for k in range(nz - 1):
        for part in range(PARTS):
            z_copies[k * PARTS + part].wait_recv()
        total = total + spread(factors[k] / safe) * z_sum[k].astype(F32)
    attended[...] = total.reshape(requests, heads_here, latent)
    outs = []
    value_load.wait()
    for h in range(heads_here):
        outs.append(jnp.dot(attended[:, h, :].astype(BF16), value_ref[h], preferred_element_type=F32).astype(BF16))
    head_out = jnp.concatenate(outs, axis=1)
    weight_load.wait()

    aligned = block % 128 == 0
    h_copies, p_copies = [], []

    def place(k):
        return (me + 1 + k) % ctx if aligned else k

    def forward(k):
        target = place(k)
        h_copies[k].wait_recv()
        merged = h_keep[k] + h_in[k]
        p_out[k] = merged.astype(BF16)
        if aligned:
            if k < ctx - 1:
                copy = remote(p_out.at[k], p_in.at[k], p_send.at[k], p_recv.at[k], {"ctx": target})
                copy.start()
                p_copies.append(copy)
        else:
            @pl.when(target != me)
            def _():
                slot = (target - me + ctx - 1) % ctx
                remote(p_out.at[k], p_in.at[slot], p_send.at[slot], p_recv.at[slot], {"ctx": target}).start()

    for k in range(ctx):
        if aligned:
            columns = weight[:, pl.ds(pl.multiple_of(place(k) * block, 128), block)]
        else:
            columns = weight[:, k * block:(k + 1) * block]
        part = jnp.dot(head_out, columns, preferred_element_type=F32)
        low, high = part[:, :half], part[:, half:]
        h_keep[k] = jnp.where(core == 0, low, high)
        h_out[k] = jnp.where(core == 0, high, low)
        copy = remote(h_out.at[k], h_in.at[k], h_send.at[k], h_recv.at[k], twin)
        copy.start()
        h_copies.append(copy)
        if k > 0:
            forward(k - 1)
    forward(ctx - 1)
    if aligned:
        result = h_keep[ctx - 1] + h_in[ctx - 1]
    else:
        result = p_out[me].astype(F32)
    for k in range(ctx - 1):
        remote(p_out.at[k], p_in.at[k], p_send.at[k], p_recv.at[k], partner).wait_recv()
        result = result + p_in[k].astype(F32)
    out_ref[...] = result.astype(BF16)
    for k in range(ctx - 1):
        remote(p_out.at[k], p_in.at[k], p_send.at[k], p_recv.at[k], partner).wait_send()
    for copy in h_copies + z_copies + z_stats + y_copies + [stat_copy]:
        copy.wait_send()
    for which in range(2):
        for part in range(PARTS):
            for origin in range(nz):
                across(which, origin, part, mine[which]).wait_send()
            for step in range(nz - 1):
                @pl.when(has_above & (z - step >= 0))
                def _():
                    upward(which, step, part, mine[which]).wait_send()

                @pl.when(has_below & (z + step < nz))
                def _():
                    downward(which, step, part, mine[which]).wait_send()


def body(ctx, query_nope, query_rope, key_absorb, value_absorb, output_weight, latent_cache, page_owner):
    requests, heads_here, nope = query_nope.shape
    latent = key_absorb.shape[2]
    rope = query_rope.shape[1] // heads_here
    page_count, page, entry = latent_cache.shape
    heads = ctx * heads_here
    cut = latent // 2
    rows = requests * heads_here
    nz = ctx // 2
    half = output_weight.shape[1] // (2 * ctx)
    wanted = -(-page_count // GROUP) + requests - 1
    unroll = min(wanted, 24)
    items = up_to(wanted, unroll)
    table_lanes = up_to(items, 128)
    vmem, dma = pltpu.VMEM, pltpu.SemaphoreType.DMA
    gather_sems = 2 * nz * PARTS
    stat_tail = (2, heads_here, 128)
    operands = [query_nope, query_rope, key_absorb, page_owner.reshape(1, page_count), latent_cache, value_absorb,
                output_weight]
    operands = [pltpu.with_memory_space_constraint(x, pltpu.HBM) for x in operands]
    return pl.pallas_call(
        functools.partial(kernel, ctx, unroll, (nope + rope) ** (-0.5)),
        out_shape=jax.ShapeDtypeStruct((requests, half), BF16),
        in_specs=[pl.BlockSpec(memory_space=pltpu.HBM)] * 7,
        out_specs=pl.BlockSpec(memory_space=pltpu.VMEM),
        scratch_shapes=[
            vmem(query_nope.shape, BF16),
            vmem(query_rope.shape, BF16),
            vmem(key_absorb.shape, BF16),
            vmem(value_absorb.shape, BF16),
            vmem(output_weight.shape, BF16),
            vmem(latent_cache.shape, BF16),
            dma((8,)),
            vmem(query_nope.shape, F32),
            vmem((requests, heads_here, cut + rope), F32),
            vmem((requests, heads_here, latent - cut), F32),
            vmem((rows, cut + rope), BF16),
            vmem((rows, latent - cut), BF16),
            vmem((ctx, rows, cut + rope), BF16),
            vmem((ctx, rows, latent - cut), BF16),
            dma((gather_sems,)), dma((gather_sems,)), dma((gather_sems,)),
            dma((gather_sems,)), dma((gather_sems,)), dma((gather_sems,)),
            vmem((1, page_count), I32),
            vmem((up_to(GROUP + 4, 8), table_lanes), I32),
            pltpu.SMEM((up_to(GROUP + 4, 8), table_lanes), I32),
            vmem((items, GROUP * page), F32),
            vmem((requests, heads, cut + rope), BF16),
            vmem((requests, heads, latent - cut), BF16),
            vmem((items, heads, GROUP * page), F32),
            vmem((items, heads, 128), F32),
            vmem((requests, heads, 128), F32),
            vmem((items, heads, latent), F32),
            vmem((2, nz, rows, latent), BF16),
            vmem((2, nz) + stat_tail, F32),
            vmem((nz, rows, latent), BF16),
            vmem((nz,) + stat_tail, F32),
            vmem((nz - 1, rows, latent), BF16),
            vmem((nz - 1,) + stat_tail, F32),
            vmem((nz - 1, rows, latent), BF16),
            vmem((nz - 1,) + stat_tail, F32),
            vmem((requests, heads_here, latent), F32),
            vmem((ctx, requests, half), F32),
            vmem((ctx, requests, half), F32),
            vmem((ctx, requests, half), F32),
            vmem((ctx, requests, half), BF16),
            vmem((ctx - 1, requests, half), BF16),
            dma((nz * PARTS,)), dma((nz * PARTS,)), dma, dma,
            dma(((nz - 1) * PARTS,)), dma(((nz - 1) * PARTS,)), dma((nz - 1,)), dma((nz - 1,)),
            dma((ctx,)), dma((ctx,)), dma((ctx - 1,)), dma((ctx - 1,)),
        ],
        compiler_params=pltpu.CompilerParams(collective_id=0, has_side_effects=True, vmem_limit_bytes=62 << 20),
    )(*operands)


def solution(mesh):
    return jax.shard_map(
        functools.partial(body, mesh.shape["ctx"]),
        mesh=mesh,
        in_specs=(
            P("groups", ("ctx", "head"), None),
            P("groups", ("ctx", "head")),
            P(("ctx", "head"), None, None),
            P(("ctx", "head"), None, None),
            P(("ctx", "head"), None),
            P(("groups", "ctx"), None, None),
            P(("groups", "ctx")),
        ),
        out_specs=P("groups", ("ctx", "head")),
        check_vma=False,
    )
```

```python
import functools

import jax
import jax.numpy as jnp
from jax import lax
from jax.experimental import pallas as pl
from jax.experimental.pallas import tpu as pltpu
from jax.sharding import PartitionSpec as P

PARTS = 2
GROUP = 4
LAG = 4
F32 = jnp.float32
BF16 = jnp.bfloat16
I32 = jnp.int32
LOW = -1e30


def dot_nt(a, b):
    return lax.dot_general(a, b, (((1,), (1,)), ((), ())), preferred_element_type=F32)


def remote(src, dst, send_sem, recv_sem, where):
    return pltpu.make_async_remote_copy(
        src_ref=src, dst_ref=dst, send_sem=send_sem, recv_sem=recv_sem,
        device_id=where, device_id_type=pl.DeviceIdType.MESH)


def up_to(n, step):
    return -(-n // step) * step


def spaced(columns):
    return (columns // 128 | 1) * 128 if columns % 128 == 0 else columns


def column(row):
    n = row.shape[1]
    diagonal = lax.broadcasted_iota(I32, (n, n), 0) == lax.broadcasted_iota(I32, (n, n), 1)
    return jnp.sum(jnp.where(diagonal, jnp.broadcast_to(row, (n, n)), 0), axis=1, keepdims=True)


def plan_items(owner, requests, group, table, bias):
    count = owner.shape[1]
    width = up_to(count, 128)
    lanes_out = table.shape[1]
    items, tokens = bias.shape
    page = tokens // group
    owner = jnp.where(owner < 0, requests, owner)
    if width > count:
        owner = jnp.concatenate([owner, jnp.full((1, width - count), requests, I32)], axis=1)
    lane = lax.broadcasted_iota(I32, (1, width), 1)
    slot = lax.broadcasted_iota(I32, (width, 1), 0)
    lanes = lax.broadcasted_iota(I32, (width, width), 1)
    places = lax.broadcasted_iota(I32, (width, width), 0)
    key = owner * width + lane
    rank = jnp.sum(jnp.where(jnp.broadcast_to(key, (width, width)) < column(key), 1, 0), axis=1, keepdims=True)
    owner_c = column(owner)
    here = rank == lanes
    order = jnp.sum(jnp.where(here, slot, 0), axis=0, keepdims=True)
    sorted_owner = jnp.sum(jnp.where(here, owner_c, 0), axis=0, keepdims=True)
    before = jnp.sum(jnp.where(rank + 1 == lanes, owner_c, 0), axis=0, keepdims=True)
    opens = (lax.rem(lane, jnp.full(lane.shape, group, I32)) == 0) | (sorted_owner != before)
    start = column(jnp.where(opens & (sorted_owner < requests), 1, 0))
    order_c, sorted_c = column(order), column(sorted_owner)
    item = column(jnp.sum(jnp.where(places <= lanes, start, 0), axis=0, keepdims=True) - 1)
    place = lax.broadcasted_iota(I32, (width, lanes_out), 0)
    mine = (item == lax.broadcasted_iota(I32, (width, lanes_out), 1)) & (start > 0)

    def pick(value):
        return jnp.sum(jnp.where(mine, value, 0), axis=0, keepdims=True)

    first, who, real = pick(slot), pick(sorted_c), pick(start)
    first = first - lax.rem(first, jnp.full(first.shape, group, I32))
    tag = jnp.where(real > 0, who, -1)
    tag_c = column(tag)
    table[0:1, :] = who
    for j in range(group):
        chosen = place == first + j
        table[1 + j:2 + j, :] = jnp.sum(jnp.where(chosen, order_c, 0), axis=0, keepdims=True)
        theirs = column(jnp.sum(jnp.where(chosen, sorted_c, 0), axis=0, keepdims=True))
        fits = jnp.where(theirs[:items] == tag_c[:items], 0.0, LOW)
        bias[:, j * page:(j + 1) * page] = jnp.broadcast_to(fits, (items, page))
    index = lax.broadcasted_iota(I32, (1, lanes_out), 1)
    previous = jnp.where(index == 0, -1, pltpu.roll(tag, 1, 1))
    table[group + 1:group + 2, :] = jnp.where(tag == previous, 1, 0)
    owned = tag_c == lax.broadcasted_iota(I32, (lanes_out, lanes_out), 1)
    number = lax.broadcasted_iota(I32, (lanes_out, lanes_out), 0)
    table[group + 2:group + 3, :] = jnp.max(jnp.where(owned, number, 0), axis=0, keepdims=True)
    table[group + 3:group + 4, :] = jnp.max(jnp.where(owned, 1, 0), axis=0, keepdims=True)


def kernel(ctx, unroll, score_scale, nope_hbm, rope_hbm, key_hbm, owner_hbm, cache_hbm, value_hbm, weight_hbm, out_ref,
           nope_ref, rope_ref, key_ref, value_ref, weight, pages, in_sems, wide, rows_a, rows_b, rows_c, mine_a, mine_b, mine_c,
           all_a, all_b, all_c, y_send, y_recv, up_send, up_recv, down_send, down_recv,
           owner_ref, table, tab, bias, query_a, query_b, query_c, scores, marks, top_full, acc,
           sums, stats, y_sum, y_stat, c_sum, c_stat, z_sum, z_stat, attended,
           h_keep, h_out, h_in, p_out, p_in,
           ys_send, ys_recv, yt_send, yt_recv, zs_send, zs_recv, zt_send, zt_recv,
           h_send, h_recv, p_send, p_recv):
    requests, heads_here, _ = nope_ref.shape
    latent = key_ref.shape[2]
    cut = query_b.shape[2]
    rope = rope_ref.shape[1] // heads_here
    items = scores.shape[0]
    nz = ctx // 2
    half = out_ref.shape[1]
    block = 2 * half
    me, core = lax.axis_index("ctx"), lax.axis_index("head")
    z, y = me // 2, me % 2
    partner, twin = {"ctx": z * 2 + 1 - y}, {"head": 1 - core}
    above, below = {"ctx": me + 2}, {"ctx": me - 2}
    has_above, has_below = z + 1 < nz, z > 0

    def load(i, src, dst):
        return pltpu.make_async_copy(src, dst, in_sems.at[i])

    first_loads = [load(0, nope_hbm, nope_ref), load(1, rope_hbm, rope_ref), load(2, key_hbm, key_ref)]
    owner_load = load(3, owner_hbm, owner_ref)
    cache_load, value_load, weight_load = (
        load(4, cache_hbm, pages), load(5, value_hbm, value_ref), load(6, weight_hbm, weight.at[:, :weight_hbm.shape[1]]))
    table_load = load(7, table, tab)
    for copy in first_loads:
        copy.start()
    owner_load.start()

    barrier = pltpu.get_barrier_semaphore()
    for k in range(1, ctx):
        pl.semaphore_signal(barrier, inc=1, device_id={"ctx": (me + k) % ctx}, device_id_type=pl.DeviceIdType.MESH)
    pl.semaphore_signal(barrier, inc=1, device_id=twin, device_id_type=pl.DeviceIdType.MESH)

    for copy in first_loads:
        copy.wait()
    cache_load.start()
    wide[...] = nope_ref[...].astype(F32)
    depth = mine_a.shape[0] // PARTS
    gathered = (all_a, all_b, all_c)

    def lines(part):
        return slice(part * depth, (part + 1) * depth)

    def block_of(which, row, part):
        return gathered[which].at[row, lines(part)]

    def sem(which, step, part):
        return (which * nz + step) * PARTS + part

    def across(which, origin, part, src=None):
        slot, i = block_of(which, origin * 2 + y, part), sem(which, origin, part)
        return remote(slot if src is None else src.at[lines(part)], slot, y_send.at[i], y_recv.at[i], partner)

    def upward(which, step, part, src=None):
        slot, i = block_of(which, me - 2 * step, part), sem(which, step, part)
        return remote(slot if src is None else src.at[lines(part)], slot, up_send.at[i], up_recv.at[i], above)

    def downward(which, step, part, src=None):
        slot, i = block_of(which, me + 2 * step, part), sem(which, step, part)
        return remote(slot if src is None else src.at[lines(part)], slot, down_send.at[i], down_recv.at[i], below)

    def arrival(which, row, part, done):
        slot = block_of(which, row, part)
        return remote(slot, slot, done, done, partner)

    mine = (mine_a, mine_b, mine_c)

    def send_along(which):
        for part in range(PARTS):
            @pl.when(has_above)
            def _():
                upward(which, 0, part, mine[which]).start()

            @pl.when(has_below)
            def _():
                downward(which, 0, part, mine[which]).start()

    def send_across(which):
        for part in range(PARTS):
            across(which, z, part, mine[which]).start()

    for h in range(heads_here):
        rows_c[:, h, :] = rope_ref[:, h * rope:(h + 1) * rope].astype(F32)
        rows_a[:, h, :] = jnp.dot(wide[:, h, :].astype(BF16), key_ref[h, :, :cut], preferred_element_type=F32)
    for which, rows in ((2, rows_c), (0, rows_a)):
        value = rows[...].reshape(requests * heads_here, rows.shape[2]).astype(BF16)
        mine[which][...] = value
        gathered[which][me] = value
    pl.semaphore_wait(barrier, ctx)
    for which in (2, 0):
        send_along(which)
        send_across(which)
    for h in range(heads_here):
        rows_b[:, h, :] = jnp.dot(wide[:, h, :].astype(BF16), key_ref[h, :, cut:], preferred_element_type=F32)
    value = rows_b[...].reshape(requests * heads_here, latent - cut).astype(BF16)
    mine_b[...] = value
    all_b[me] = value
    send_along(1)
    send_across(1)
    value_load.start()
    weight_load.start()

    owner_load.wait()
    plan_items(owner_ref[...], requests, GROUP, table, bias)
    table_load.start()

    def pass_on(which, step):
        for part in range(PARTS):
            @pl.when(z - 1 - step >= 0)
            def _():
                arrival(which, me - 2 * (step + 1), part, up_recv.at[sem(which, step, part)]).wait_recv()
                if step + 1 < nz - 1:
                    @pl.when(has_above)
                    def _():
                        upward(which, step + 1, part).start()
                across(which, z - 1 - step, part).start()

            @pl.when(z + 1 + step < nz)
            def _():
                arrival(which, me + 2 * (step + 1), part, down_recv.at[sem(which, step, part)]).wait_recv()
                if step + 1 < nz - 1:
                    @pl.when(has_below)
                    def _():
                        downward(which, step + 1, part).start()
                across(which, z + 1 + step, part).start()

    for step in range(nz - 1):
        pass_on(2, step)
        pass_on(0, step)
        if 1 <= step < nz - 2:
            pass_on(1, step - 1)

    def settle(which, query):
        for origin in range(nz):
            for part in range(PARTS):
                arrival(which, origin * 2 + 1 - y, part, y_recv.at[sem(which, origin, part)]).wait_recv()
        for r in range(requests):
            lots = [gathered[which][c, r * heads_here:(r + 1) * heads_here, :].astype(F32) for c in range(ctx)]
            query[r] = jnp.concatenate(lots, axis=0).astype(BF16)

    table_load.wait()
    cache_load.wait()

    def entries(i, columns):
        return jnp.concatenate([pages[tab[1 + j, i], :, columns] for j in range(GROUP)], axis=0)

    def rope_scores(s, carry):
        for u in range(unroll):
            i = s * unroll + u
            scores[i] = dot_nt(query_c[tab[0, i]], entries(i, slice(latent, latent + rope)))
        return carry

    def first_scores(s, carry):
        for u in range(unroll):
            i = s * unroll + u
            scores[i] = scores[i] + dot_nt(query_a[tab[0, i]], entries(i, slice(0, cut)))
        return carry

    settle(2, query_c)
    slices = items // unroll
    left = [step for step in range(nz - 1) if step == nz - 2 or step == nz - 3]
    for n in range(slices):
        lax.fori_loop(n, n + 1, rope_scores, 0)
        if n < len(left) and n < slices - 1:
            pass_on(1, left[n])
    for step in left[slices - 1:]:
        pass_on(1, step)
    settle(0, query_a)
    lax.fori_loop(0, slices, first_scores, 0)
    settle(1, query_b)

    def last_scores(s, top):
        for u in range(unroll):
            i = s * unroll + u
            found = scores[i] + dot_nt(query_b[tab[0, i]], entries(i, slice(cut, latent)))
            found = found * score_scale + bias[pl.ds(i, 1), :]
            scores[i] = found
            top = jnp.where(tab[GROUP + 1, i] > 0, top, LOW)
            for j in range(found.shape[1] // 128):
                top = jnp.maximum(top, found[:, j * 128:(j + 1) * 128])
            marks[i] = top
        return top

    lax.fori_loop(0, items // unroll, last_scores, jnp.full(marks.shape[1:], LOW, F32))
    for r in range(requests):
        seen = marks[tab[GROUP + 2, r]]
        top_full[r] = jnp.broadcast_to(jnp.max(seen, axis=1, keepdims=True), seen.shape)

    def weigh(s, carry):
        total, held = carry
        for u in range(unroll):
            i = s * unroll + u
            keep = tab[GROUP + 1, i] > 0
            top = top_full[tab[0, i]]
            total = jnp.where(keep, total, 0.0)
            weights = []
            for j in range(scores.shape[2] // 128):
                weight_j = jnp.exp(scores[i, :, j * 128:(j + 1) * 128] - top)
                total = total + weight_j
                weights.append(weight_j.astype(BF16))
            marks[i] = total
            held = jnp.where(keep, held, 0.0) + jnp.dot(
                jnp.concatenate(weights, axis=1), entries(i, slice(0, latent)), preferred_element_type=F32)
            acc[i] = held
        return total, held

    lax.fori_loop(0, items // unroll, weigh, (jnp.zeros(marks.shape[1:], F32), jnp.zeros(acc.shape[1:], F32)))

    lane = lax.broadcasted_iota(I32, marks.shape[1:], 1)
    top = jnp.full(lane.shape, LOW, F32)
    norm = jnp.zeros(lane.shape, F32)
    for r in range(requests):
        here = (lane == r) & jnp.broadcast_to(tab[GROUP + 3, r] > 0, lane.shape)
        top = jnp.where(here, top_full[r], top)
        norm = jnp.where(here, jnp.sum(marks[tab[GROUP + 2, r]], axis=1, keepdims=True), norm)
    for c in range(ctx):
        rows = slice(c * heads_here, (c + 1) * heads_here)
        stats[c % 2, c // 2, 0] = top[rows]
        stats[c % 2, c // 2, 1] = norm[rows]
        lots = [acc[tab[GROUP + 2, r], rows, :] for r in range(requests)]
        sums[c % 2, c // 2] = jnp.concatenate(lots, axis=0).astype(BF16)

    def opposite(k):
        return z ^ (nz - 1 - k) if nz & (nz - 1) == 0 else (z + 1 + k) % nz

    stat_copy = remote(stats.at[1 - y], y_stat, yt_send, yt_recv, partner)
    stat_copy.start()
    y_copies = []
    for k in range(nz):
        target = opposite(k)
        for part in range(PARTS):
            i = k * PARTS + part
            copy = remote(sums.at[1 - y, target, lines(part)], y_sum.at[k, lines(part)],
                          ys_send.at[i], ys_recv.at[i], partner)
            copy.start()
            y_copies.append(copy)
    stat_copy.wait_recv()

    def spread(factor):
        return jnp.concatenate([factor[:, r:r + 1] for r in range(requests)], axis=0)

    z_copies, z_stats = [], []
    for k in range(nz):
        target = opposite(k)
        top_a, norm_a = stats[y, target, 0], stats[y, target, 1]
        top_b, norm_b = y_stat[target, 0], y_stat[target, 1]
        top = jnp.maximum(top_a, top_b)
        keep_a, keep_b = jnp.exp(top_a - top), jnp.exp(top_b - top)
        norm = keep_a * norm_a + keep_b * norm_b
        rows_x, rows_y = spread(keep_a), spread(keep_b)
        there = {"ctx": target * 2 + y}
        if k < nz - 1:
            c_stat[k, 0] = top
            c_stat[k, 1] = norm
            copy = remote(c_stat.at[k], z_stat.at[k], zt_send.at[k], zt_recv.at[k], there)
            copy.start()
            z_stats.append(copy)
        both = []
        for part in range(PARTS):
            i = k * PARTS + part
            y_copies[i].wait_recv()
            both.append(rows_x[lines(part)] * sums[y, target, lines(part)].astype(F32)
                        + rows_y[lines(part)] * y_sum[k, lines(part)].astype(F32))
            if k < nz - 1:
                c_sum[k, lines(part)] = both[part].astype(BF16)
                copy = remote(c_sum.at[k, lines(part)], z_sum.at[k, lines(part)], zs_send.at[i], zs_recv.at[i], there)
                copy.start()
                z_copies.append(copy)
    both = jnp.concatenate(both, axis=0)
    for copy in z_stats:
        copy.wait_recv()
    highest = top
    for k in range(nz - 1):
        highest = jnp.maximum(highest, z_stat[k, 0])
    keep = jnp.exp(top - highest)
    all_norm = keep * norm
    factors = []
    for k in range(nz - 1):
        factors.append(jnp.exp(z_stat[k, 0] - highest))
        all_norm = all_norm + factors[k] * z_stat[k, 1]
    safe = jnp.where(all_norm > 0, all_norm, 1.0)
    total = spread(keep / safe) * both
    for k in range(nz - 1):
        for part in range(PARTS):
            z_copies[k * PARTS + part].wait_recv()
        total = total + spread(factors[k] / safe) * z_sum[k].astype(F32)
    attended[...] = total.reshape(requests, heads_here, latent)
    outs = []
    value_load.wait()
    for h in range(heads_here):
        outs.append(jnp.dot(attended[:, h, :].astype(BF16), value_ref[h], preferred_element_type=F32).astype(BF16))
    head_out = jnp.concatenate(outs, axis=1)
    weight_load.wait()

    aligned = block % 128 == 0
    h_copies, p_copies = [], []

    def place(k):
        if not aligned:
            return k
        return me ^ (ctx - 1 - k) if ctx & (ctx - 1) == 0 else (me + 1 + k) % ctx

    def forward(k):
        target = place(k)
        h_copies[k].wait_recv()
        merged = h_keep[k] + h_in[k]
        p_out[k] = merged.astype(BF16)
        if aligned:
            if k < ctx - 1:
                copy = remote(p_out.at[k], p_in.at[k], p_send.at[k], p_recv.at[k], {"ctx": target})
                copy.start()
                p_copies.append(copy)
        else:
            @pl.when(target != me)
            def _():
                slot = (target - me + ctx - 1) % ctx
                remote(p_out.at[k], p_in.at[slot], p_send.at[slot], p_recv.at[slot], {"ctx": target}).start()

    for k in range(ctx):
        if aligned:
            columns = weight[:, pl.ds(pl.multiple_of(place(k) * block, 128), block)]
        else:
            columns = weight[:, k * block:(k + 1) * block]
        part = jnp.dot(head_out, columns, preferred_element_type=F32)
        low, high = part[:, :half], part[:, half:]
        h_keep[k] = jnp.where(core == 0, low, high)
        h_out[k] = jnp.where(core == 0, high, low)
        copy = remote(h_out.at[k], h_in.at[k], h_send.at[k], h_recv.at[k], twin)
        copy.start()
        h_copies.append(copy)
        if k >= LAG:
            forward(k - LAG)
    for k in range(max(ctx - LAG, 0), ctx):
        forward(k)
    if aligned:
        result = h_keep[ctx - 1] + h_in[ctx - 1]
    else:
        result = p_out[me].astype(F32)
    for k in range(ctx - 1):
        remote(p_out.at[k], p_in.at[k], p_send.at[k], p_recv.at[k], partner).wait_recv()
        result = result + p_in[k].astype(F32)
    out_ref[...] = result.astype(BF16)
    for k in range(ctx - 1):
        remote(p_out.at[k], p_in.at[k], p_send.at[k], p_recv.at[k], partner).wait_send()
    for copy in h_copies + z_copies + z_stats + y_copies + [stat_copy]:
        copy.wait_send()
    for which in range(3):
        for part in range(PARTS):
            for origin in range(nz):
                across(which, origin, part, mine[which]).wait_send()
            for step in range(nz - 1):
                @pl.when(has_above & (z - step >= 0))
                def _():
                    upward(which, step, part, mine[which]).wait_send()

                @pl.when(has_below & (z + step < nz))
                def _():
                    downward(which, step, part, mine[which]).wait_send()


def body(ctx, query_nope, query_rope, key_absorb, value_absorb, output_weight, latent_cache, page_owner):
    requests, heads_here, nope = query_nope.shape
    latent = key_absorb.shape[2]
    rope = query_rope.shape[1] // heads_here
    page_count, page, entry = latent_cache.shape
    heads = ctx * heads_here
    cut = latent // 2
    rows = requests * heads_here
    nz = ctx // 2
    half = output_weight.shape[1] // (2 * ctx)
    wanted = -(-page_count // GROUP) + requests - 1
    unroll = min(wanted, 24)
    items = up_to(wanted, unroll)
    table_lanes = up_to(items, 128)
    vmem, dma = pltpu.VMEM, pltpu.SemaphoreType.DMA
    gather_sems = 3 * nz * PARTS
    stat_tail = (2, heads_here, 128)
    operands = [query_nope, query_rope, key_absorb, page_owner.reshape(1, page_count), latent_cache, value_absorb,
                output_weight]
    operands = [pltpu.with_memory_space_constraint(x, pltpu.HBM) for x in operands]
    return pl.pallas_call(
        functools.partial(kernel, ctx, unroll, (nope + rope) ** (-0.5)),
        out_shape=jax.ShapeDtypeStruct((requests, half), BF16),
        in_specs=[pl.BlockSpec(memory_space=pltpu.HBM)] * 7,
        out_specs=pl.BlockSpec(memory_space=pltpu.VMEM),
        scratch_shapes=[
            vmem(query_nope.shape, BF16),
            vmem(query_rope.shape, BF16),
            vmem(key_absorb.shape, BF16),
            vmem(value_absorb.shape, BF16),
            vmem((output_weight.shape[0], spaced(output_weight.shape[1])), BF16),
            vmem(latent_cache.shape, BF16),
            dma((8,)),
            vmem(query_nope.shape, F32),
            vmem((requests, heads_here, cut), F32),
            vmem((requests, heads_here, latent - cut), F32),
            vmem((requests, heads_here, rope), F32),
            vmem((rows, cut), BF16),
            vmem((rows, latent - cut), BF16),
            vmem((rows, rope), BF16),
            vmem((ctx, rows, cut), BF16),
            vmem((ctx, rows, latent - cut), BF16),
            vmem((ctx, rows, rope), BF16),
            dma((gather_sems,)), dma((gather_sems,)), dma((gather_sems,)),
            dma((gather_sems,)), dma((gather_sems,)), dma((gather_sems,)),
            vmem((1, page_count), I32),
            vmem((up_to(GROUP + 4, 8), table_lanes), I32),
            pltpu.SMEM((up_to(GROUP + 4, 8), table_lanes), I32),
            vmem((items, GROUP * page), F32),
            vmem((requests, heads, cut), BF16),
            vmem((requests, heads, latent - cut), BF16),
            vmem((requests, heads, rope), BF16),
            vmem((items, heads, GROUP * page), F32),
            vmem((items, heads, 128), F32),
            vmem((requests, heads, 128), F32),
            vmem((items, heads, latent), F32),
            vmem((2, nz, rows, latent), BF16),
            vmem((2, nz) + stat_tail, F32),
            vmem((nz, rows, latent), BF16),
            vmem((nz,) + stat_tail, F32),
            vmem((nz - 1, rows, latent), BF16),
            vmem((nz - 1,) + stat_tail, F32),
            vmem((nz - 1, rows, latent), BF16),
            vmem((nz - 1,) + stat_tail, F32),
            vmem((requests, heads_here, latent), F32),
            vmem((ctx, requests, half), F32),
            vmem((ctx, requests, half), F32),
            vmem((ctx, requests, half), F32),
            vmem((ctx, requests, half), BF16),
            vmem((ctx - 1, requests, half), BF16),
            dma((nz * PARTS,)), dma((nz * PARTS,)), dma, dma,
            dma(((nz - 1) * PARTS,)), dma(((nz - 1) * PARTS,)), dma((nz - 1,)), dma((nz - 1,)),
            dma((ctx,)), dma((ctx,)), dma((ctx - 1,)), dma((ctx - 1,)),
        ],
        compiler_params=pltpu.CompilerParams(collective_id=0, has_side_effects=True, vmem_limit_bytes=62 << 20),
    )(*operands)


def solution(mesh):
    return jax.shard_map(
        functools.partial(body, mesh.shape["ctx"]),
        mesh=mesh,
        in_specs=(
            P("groups", ("ctx", "head"), None),
            P("groups", ("ctx", "head")),
            P(("ctx", "head"), None, None),
            P(("ctx", "head"), None, None),
            P(("ctx", "head"), None),
            P(("groups", "ctx"), None, None),
            P(("groups", "ctx")),
        ),
        out_specs=P("groups", ("ctx", "head")),
        check_vma=False,
    )
```

```python
import functools

import jax
import jax.numpy as jnp
from jax import lax
from jax.experimental import pallas as pl
from jax.experimental.pallas import tpu as pltpu
from jax.sharding import PartitionSpec as P

PARTS = 2
FIRST, SECOND, ROTARY = range(3)
GROUP = 4
BATCH = 3
UNROLLED = 2
F32 = jnp.float32
BF16 = jnp.bfloat16
I32 = jnp.int32
LOW = -1e30


def dot_nt(a, b):
    return lax.dot_general(a, b, (((1,), (1,)), ((), ())), preferred_element_type=F32)


def remote(src, dst, send_sem, recv_sem, where):
    return pltpu.make_async_remote_copy(
        src_ref=src, dst_ref=dst, send_sem=send_sem, recv_sem=recv_sem,
        device_id=where, device_id_type=pl.DeviceIdType.MESH)


def up_to(n, step):
    return -(-n // step) * step


def spaced(columns):
    return (columns // 128 | 1) * 128 if columns % 128 == 0 else columns


def column(row):
    n = row.shape[1]
    diagonal = lax.broadcasted_iota(I32, (n, n), 0) == lax.broadcasted_iota(I32, (n, n), 1)
    return jnp.sum(jnp.where(diagonal, jnp.broadcast_to(row, (n, n)), 0), axis=1, keepdims=True)


def plan_items(owner, requests, group, table, bias):
    count = owner.shape[1]
    width = up_to(count, 128)
    lanes_out = table.shape[1]
    items, tokens = bias.shape
    page = tokens // group
    owner = jnp.where(owner < 0, requests, owner)
    if width > count:
        owner = jnp.concatenate([owner, jnp.full((1, width - count), requests, I32)], axis=1)
    lane = lax.broadcasted_iota(I32, (1, width), 1)
    slot = lax.broadcasted_iota(I32, (width, 1), 0)
    lanes = lax.broadcasted_iota(I32, (width, width), 1)
    places = lax.broadcasted_iota(I32, (width, width), 0)
    key = owner * width + lane
    rank = jnp.sum(jnp.where(jnp.broadcast_to(key, (width, width)) < column(key), 1, 0), axis=1, keepdims=True)
    owner_c = column(owner)
    here = rank == lanes
    order = jnp.sum(jnp.where(here, slot, 0), axis=0, keepdims=True)
    sorted_owner = jnp.sum(jnp.where(here, owner_c, 0), axis=0, keepdims=True)
    sorted_c = column(sorted_owner)
    ahead = jnp.sum(jnp.where(sorted_c < sorted_owner, 1, 0), axis=0, keepdims=True)
    opens = lax.rem(lane - ahead, jnp.full(lane.shape, group, I32)) == 0
    start = column(jnp.where(opens & (sorted_owner < requests), 1, 0))
    order_c = jnp.minimum(column(order), count - 1)
    item = column(jnp.sum(jnp.where(places <= lanes, start, 0), axis=0, keepdims=True) - 1)
    place = lax.broadcasted_iota(I32, (width, lanes_out), 0)
    mine = (item == lax.broadcasted_iota(I32, (width, lanes_out), 1)) & (start > 0)

    def pick(value):
        return jnp.sum(jnp.where(mine, value, 0), axis=0, keepdims=True)

    first, who, real = pick(slot), pick(sorted_c), pick(start)
    tag = jnp.where(real > 0, who, -1)
    tag_c = column(tag)
    table[0:1, :] = who
    for j in range(group):
        chosen = place == first + j
        table[1 + j:2 + j, :] = jnp.sum(jnp.where(chosen, order_c, 0), axis=0, keepdims=True)
        theirs = column(jnp.sum(jnp.where(chosen, sorted_c + 1, 0), axis=0, keepdims=True) - 1)
        fits = jnp.where(theirs[:items] == tag_c[:items], 0.0, LOW)
        bias[:, j * page:(j + 1) * page] = jnp.broadcast_to(fits, (items, page))
    index = lax.broadcasted_iota(I32, (1, lanes_out), 1)
    previous = jnp.where(index == 0, -1, pltpu.roll(tag, 1, 1))
    table[group + 1:group + 2, :] = jnp.where(tag == previous, 1, 0)
    owned = tag_c == lax.broadcasted_iota(I32, (lanes_out, lanes_out), 1)
    number = lax.broadcasted_iota(I32, (lanes_out, lanes_out), 0)
    table[group + 2:group + 3, :] = jnp.max(jnp.where(owned, number, 0), axis=0, keepdims=True)
    table[group + 3:group + 4, :] = jnp.max(jnp.where(owned, 1, 0), axis=0, keepdims=True)


def kernel(ctx, unroll, score_scale, nope_hbm, rope_hbm, key_hbm, owner_hbm, cache_hbm, value_hbm, weight_hbm, out_ref,
           nope_ref, rope_ref, key_ref, value_ref, weight, pages, in_sems, wide, rows_a, rows_b, rows_c, mine_a, mine_b,
           all_a, all_b, all_c, y_send, y_recv, up_send, up_recv, down_send, down_recv,
           owner_ref, table, tab, bias, query_a, query_b, query_c, scores, marks, top_full, acc,
           sums, stats, y_sum, y_stat, c_sum, c_stat, z_sum, z_stat, attended,
           p_out, p_in,
           ys_send, ys_recv, yt_send, yt_recv, zs_send, zs_recv, zt_send, zt_recv,
           p_send, p_recv):
    requests, heads_here, _ = nope_ref.shape
    latent = key_ref.shape[2]
    cut = query_b.shape[2]
    rope = rope_ref.shape[1] // heads_here
    items = scores.shape[0]
    nz = ctx // 2
    half = out_ref.shape[1]
    block = 2 * half
    me, core = lax.axis_index("ctx"), lax.axis_index("head")
    z, y = me // 2, me % 2
    partner, twin = {"ctx": z * 2 + 1 - y}, {"head": 1 - core}
    above, below = {"ctx": me + 2}, {"ctx": me - 2}
    has_above, has_below = z + 1 < nz, z > 0

    def load(i, src, dst):
        return pltpu.make_async_copy(src, dst, in_sems.at[i])

    first_loads = [load(0, nope_hbm, nope_ref), load(1, rope_hbm, rope_ref), load(2, key_hbm, key_ref)]
    owner_load = load(3, owner_hbm, owner_ref)
    cache_load, value_load, weight_load = (
        load(4, cache_hbm, pages), load(5, value_hbm, value_ref), load(6, weight_hbm, weight.at[:, :weight_hbm.shape[1]]))
    table_load = load(7, table, tab)
    for copy in first_loads:
        copy.start()
    owner_load.start()

    barrier = pltpu.get_barrier_semaphore()
    for k in range(1, ctx):
        pl.semaphore_signal(barrier, inc=1, device_id={"ctx": (me + k) % ctx}, device_id_type=pl.DeviceIdType.MESH)
        pl.semaphore_signal(barrier, inc=1, device_id={"ctx": (me + k) % ctx, "head": 1 - core},
                            device_id_type=pl.DeviceIdType.MESH)
    pl.semaphore_signal(barrier, inc=1, device_id=twin, device_id_type=pl.DeviceIdType.MESH)

    for copy in first_loads:
        copy.wait()
    cache_load.start()
    wide[...] = nope_ref[...].astype(F32)
    depth = mine_a.shape[0] // PARTS
    gathered = (all_a, all_b, all_c)

    def lines(part):
        return slice(part * depth, (part + 1) * depth)

    def parts(which):
        return range(1 if which == ROTARY else PARTS)

    def piece(which, part):
        return slice(0, requests) if which == ROTARY else lines(part)

    def block_of(which, row, part):
        return gathered[which].at[row, piece(which, part)]

    def sem(which, step, part):
        return (which * nz + step) * PARTS + part

    def across(which, origin, part, src=None):
        slot, i = block_of(which, origin * 2 + y, part), sem(which, origin, part)
        return remote(slot if src is None else src.at[piece(which, part)], slot, y_send.at[i], y_recv.at[i], partner)

    def upward(which, step, part, src=None):
        slot, i = block_of(which, me - 2 * step, part), sem(which, step, part)
        return remote(slot if src is None else src.at[piece(which, part)], slot, up_send.at[i], up_recv.at[i], above)

    def downward(which, step, part, src=None):
        slot, i = block_of(which, me + 2 * step, part), sem(which, step, part)
        return remote(slot if src is None else src.at[piece(which, part)], slot, down_send.at[i], down_recv.at[i], below)

    def arrival(which, row, part, done):
        slot = block_of(which, row, part)
        return remote(slot, slot, done, done, partner)

    mine = (mine_a, mine_b, rope_ref)

    def send_along(which):
        for part in parts(which):
            @pl.when(has_above)
            def _():
                upward(which, 0, part, mine[which]).start()

            @pl.when(has_below)
            def _():
                downward(which, 0, part, mine[which]).start()

    def send_across(which):
        for part in parts(which):
            across(which, z, part, mine[which]).start()

    all_c[me] = rope_ref[...]
    for h in range(heads_here):
        rows_a[:, h, :] = jnp.dot(wide[:, h, :].astype(BF16), key_ref[h, :, :cut], preferred_element_type=F32)
    value = rows_a[...].reshape(requests * heads_here, cut).astype(BF16)
    mine_a[...] = value
    all_a[me] = value
    pl.semaphore_wait(barrier, 2 * ctx - 1)
    for which in (2, 0):
        send_along(which)
        send_across(which)
    for h in range(heads_here):
        rows_b[:, h, :] = jnp.dot(wide[:, h, :].astype(BF16), key_ref[h, :, cut:], preferred_element_type=F32)
    value = rows_b[...].reshape(requests * heads_here, latent - cut).astype(BF16)
    mine_b[...] = value
    all_b[me] = value
    send_along(1)
    send_across(1)
    value_load.start()
    weight_load.start()

    owner_load.wait()
    plan_items(owner_ref[...], requests, GROUP, table, bias)
    table_load.start()

    def pass_on(which, step):
        for part in parts(which):
            @pl.when(z - 1 - step >= 0)
            def _():
                arrival(which, me - 2 * (step + 1), part, up_recv.at[sem(which, step, part)]).wait_recv()
                if step + 1 < nz - 1:
                    @pl.when(has_above)
                    def _():
                        upward(which, step + 1, part).start()
                across(which, z - 1 - step, part).start()

            @pl.when(z + 1 + step < nz)
            def _():
                arrival(which, me + 2 * (step + 1), part, down_recv.at[sem(which, step, part)]).wait_recv()
                if step + 1 < nz - 1:
                    @pl.when(has_below)
                    def _():
                        downward(which, step + 1, part).start()
                across(which, z + 1 + step, part).start()

    for step in range(nz - 1):
        pass_on(2, step)
        pass_on(0, step)
        if 1 <= step < nz - 2:
            pass_on(1, step - 1)

    def settle(which, query):
        for origin in range(nz):
            for part in parts(which):
                arrival(which, origin * 2 + 1 - y, part, y_recv.at[sem(which, origin, part)]).wait_recv()
        if which == ROTARY:
            for c in range(ctx):
                for h in range(heads_here):
                    rows_c[:, c * heads_here + h, :] = all_c[c, :, h * rope:(h + 1) * rope].astype(F32)
            query[...] = rows_c[...].astype(BF16)
            return
        for r in range(requests):
            lots = [gathered[which][c, r * heads_here:(r + 1) * heads_here, :].astype(F32) for c in range(ctx)]
            query[r] = jnp.concatenate(lots, axis=0).astype(BF16)

    table_load.wait()
    cache_load.wait()

    def entries(i, columns):
        return jnp.concatenate([pages[tab[1 + j, i], :, columns] for j in range(GROUP)], axis=0)

    def rope_scores(s, carry):
        for u in range(unroll):
            i = s * unroll + u
            scores[i] = dot_nt(query_c[tab[0, i]], entries(i, slice(latent, latent + rope)))
        return carry

    def first_scores(s, carry):
        for u in range(unroll):
            i = s * unroll + u
            scores[i] = scores[i] + dot_nt(query_a[tab[0, i]], entries(i, slice(0, cut)))
        return carry

    settle(2, query_c)
    slices = items // unroll
    left = [step for step in range(nz - 1) if step == nz - 2 or step == nz - 3]
    for n in range(slices):
        lax.fori_loop(n, n + 1, rope_scores, 0)
        if n < len(left) and n < slices - 1:
            pass_on(1, left[n])
    for step in left[slices - 1:]:
        pass_on(1, step)
    settle(0, query_a)
    lax.fori_loop(0, slices, first_scores, 0)
    settle(1, query_b)

    def last_scores(s, top):
        for u in range(unroll):
            i = s * unroll + u
            found = scores[i] + dot_nt(query_b[tab[0, i]], entries(i, slice(cut, latent)))
            found = found * score_scale + bias[pl.ds(i, 1), :]
            scores[i] = found
            top = jnp.where(tab[GROUP + 1, i] > 0, top, LOW)
            for j in range(found.shape[1] // 128):
                top = jnp.maximum(top, found[:, j * 128:(j + 1) * 128])
            marks[i] = top
        return top

    lax.fori_loop(0, items // unroll, last_scores, jnp.full(marks.shape[1:], LOW, F32))
    for r in range(requests):
        seen = marks[tab[GROUP + 2, r]]
        top_full[r] = jnp.broadcast_to(jnp.max(seen, axis=1, keepdims=True), seen.shape)

    def weigh(s, carry):
        total, held = carry
        for u in range(unroll):
            i = s * unroll + u
            keep = tab[GROUP + 1, i] > 0
            top = top_full[tab[0, i]]
            total = jnp.where(keep, total, 0.0)
            weights = []
            for j in range(scores.shape[2] // 128):
                weight_j = jnp.exp(scores[i, :, j * 128:(j + 1) * 128] - top)
                total = total + weight_j
                weights.append(weight_j.astype(BF16))
            marks[i] = total
            held = jnp.where(keep, held, 0.0) + jnp.dot(
                jnp.concatenate(weights, axis=1), entries(i, slice(0, latent)), preferred_element_type=F32)
            acc[i] = held
        return total, held

    lax.fori_loop(0, items // unroll, weigh, (jnp.zeros(marks.shape[1:], F32), jnp.zeros(acc.shape[1:], F32)))

    lane = lax.broadcasted_iota(I32, marks.shape[1:], 1)
    top = jnp.full(lane.shape, LOW, F32)
    norm = jnp.zeros(lane.shape, F32)
    for r in range(requests):
        here = (lane == r) & jnp.broadcast_to(tab[GROUP + 3, r] > 0, lane.shape)
        top = jnp.where(here, top_full[r], top)
        norm = jnp.where(here, jnp.sum(marks[tab[GROUP + 2, r]], axis=1, keepdims=True), norm)
    for c in range(ctx):
        rows = slice(c * heads_here, (c + 1) * heads_here)
        stats[c % 2, c // 2, 0] = top[rows]
        stats[c % 2, c // 2, 1] = norm[rows]
        lots = [acc[tab[GROUP + 2, r], rows, :] for r in range(requests)]
        sums[c % 2, c // 2] = jnp.concatenate(lots, axis=0).astype(BF16)

    def opposite(k):
        return z ^ (nz - 1 - k) if nz & (nz - 1) == 0 else (z + 1 + k) % nz

    stat_copy = remote(stats.at[1 - y], y_stat, yt_send, yt_recv, partner)
    stat_copy.start()
    y_copies = []
    for k in range(nz):
        target = opposite(k)
        for part in range(PARTS):
            i = k * PARTS + part
            copy = remote(sums.at[1 - y, target, lines(part)], y_sum.at[k, lines(part)],
                          ys_send.at[i], ys_recv.at[i], partner)
            copy.start()
            y_copies.append(copy)
    stat_copy.wait_recv()

    def spread(factor):
        return jnp.concatenate([factor[:, r:r + 1] for r in range(requests)], axis=0)

    z_copies, z_stats = [], []
    for k in range(nz):
        target = opposite(k)
        top_a, norm_a = stats[y, target, 0], stats[y, target, 1]
        top_b, norm_b = y_stat[target, 0], y_stat[target, 1]
        top = jnp.maximum(top_a, top_b)
        keep_a, keep_b = jnp.exp(top_a - top), jnp.exp(top_b - top)
        norm = keep_a * norm_a + keep_b * norm_b
        rows_x, rows_y = spread(keep_a), spread(keep_b)
        there = {"ctx": target * 2 + y}
        if k < nz - 1:
            c_stat[k, 0] = top
            c_stat[k, 1] = norm
            copy = remote(c_stat.at[k], z_stat.at[k], zt_send.at[k], zt_recv.at[k], there)
            copy.start()
            z_stats.append(copy)
        both = []
        for part in range(PARTS):
            i = k * PARTS + part
            y_copies[i].wait_recv()
            both.append(rows_x[lines(part)] * sums[y, target, lines(part)].astype(F32)
                        + rows_y[lines(part)] * y_sum[k, lines(part)].astype(F32))
            if k < nz - 1:
                c_sum[k, lines(part)] = both[part].astype(BF16)
                copy = remote(c_sum.at[k, lines(part)], z_sum.at[k, lines(part)], zs_send.at[i], zs_recv.at[i], there)
                copy.start()
                z_copies.append(copy)
    both = jnp.concatenate(both, axis=0)
    for copy in z_stats:
        copy.wait_recv()
    highest = top
    for k in range(nz - 1):
        highest = jnp.maximum(highest, z_stat[k, 0])
    keep = jnp.exp(top - highest)
    all_norm = keep * norm
    factors = []
    for k in range(nz - 1):
        factors.append(jnp.exp(z_stat[k, 0] - highest))
        all_norm = all_norm + factors[k] * z_stat[k, 1]
    safe = jnp.where(all_norm > 0, all_norm, 1.0)
    total = spread(keep / safe) * both
    for k in range(nz - 1):
        for part in range(PARTS):
            z_copies[k * PARTS + part].wait_recv()
        total = total + spread(factors[k] / safe) * z_sum[k].astype(F32)
    attended[...] = total.reshape(requests, heads_here, latent)
    outs = []
    value_load.wait()
    for h in range(heads_here):
        outs.append(jnp.dot(attended[:, h, :].astype(BF16), value_ref[h], preferred_element_type=F32).astype(BF16))
    head_out = jnp.concatenate(outs, axis=1)
    weight_load.wait()

    aligned = block % 128 == 0
    powers = ctx & (ctx - 1) == 0
    own = ctx - 1 if aligned else 0

    def place(k):
        if not aligned:
            return k
        return me ^ (ctx - 1 - k) if powers else (me + 1 + k) % ctx

    def send_out(k, side):
        target = place(k)
        slot = (k if aligned else (target - me + ctx) % ctx) * 2 + core
        return remote(p_out.at[k * 2 + side], p_in.at[slot], p_send.at[k * 2 + side], p_recv.at[slot],
                      {"ctx": target, "head": side})

    def each_out(k, act):
        for side in range(2):
            if aligned and k != own:
                act(send_out(k, side))
            else:
                @pl.when((place(k) != me) | (core != side))
                def _():
                    act(send_out(k, side))

    for base in range(0, ctx, BATCH):
        batch = range(base, min(base + BATCH, ctx))
        for k in batch:
            if aligned:
                columns = weight[:, pl.ds(pl.multiple_of(place(k) * block, 128), block)]
            else:
                columns = weight[:, k * block:(k + 1) * block]
            part = jnp.dot(head_out, columns, preferred_element_type=F32).astype(BF16)
            p_out[k * 2] = part[:, :half]
            p_out[k * 2 + 1] = part[:, half:]
        for k in batch:
            each_out(k, lambda copy: copy.start())
    result = p_out[(own if aligned else me) * 2 + core].astype(F32)
    for k in range(ctx):
        for side in range(2):
            slot = k * 2 + side
            if k != own:
                remote(p_in.at[slot], p_in.at[slot], p_recv.at[slot], p_recv.at[slot], twin).wait_recv()
                result = result + p_in[slot].astype(F32)
    far = own * 2 + 1 - core
    remote(p_in.at[far], p_in.at[far], p_recv.at[far], p_recv.at[far], twin).wait_recv()
    result = result + p_in[far].astype(F32)
    out_ref[...] = result.astype(BF16)
    for k in range(ctx):
        each_out(k, lambda copy: copy.wait_send())
    for copy in z_copies + z_stats + y_copies + [stat_copy]:
        copy.wait_send()
    for which in (FIRST, SECOND, ROTARY):
        for part in parts(which):
            for origin in range(nz):
                across(which, origin, part, mine[which]).wait_send()
            for step in range(nz - 1):
                @pl.when(has_above & (z - step >= 0))
                def _():
                    upward(which, step, part, mine[which]).wait_send()

                @pl.when(has_below & (z + step < nz))
                def _():
                    downward(which, step, part, mine[which]).wait_send()


def body(ctx, query_nope, query_rope, key_absorb, value_absorb, output_weight, latent_cache, page_owner):
    requests, heads_here, nope = query_nope.shape
    latent = key_absorb.shape[2]
    rope = query_rope.shape[1] // heads_here
    page_count, page, entry = latent_cache.shape
    heads = ctx * heads_here
    cut = latent // 2
    rows = requests * heads_here
    nz = ctx // 2
    half = output_weight.shape[1] // (2 * ctx)
    wanted = (page_count + (GROUP - 1) * requests) // GROUP
    unroll = -(-wanted // UNROLLED)
    items = up_to(wanted, unroll)
    table_lanes = up_to(items, 128)
    vmem, dma = pltpu.VMEM, pltpu.SemaphoreType.DMA
    gather_sems = 3 * nz * PARTS
    stat_tail = (2, heads_here, 128)
    operands = [query_nope, query_rope, key_absorb, page_owner.reshape(1, page_count), latent_cache, value_absorb,
                output_weight]
    operands = [pltpu.with_memory_space_constraint(x, pltpu.HBM) for x in operands]
    return pl.pallas_call(
        functools.partial(kernel, ctx, unroll, (nope + rope) ** (-0.5)),
        out_shape=jax.ShapeDtypeStruct((requests, half), BF16),
        in_specs=[pl.BlockSpec(memory_space=pltpu.HBM)] * 7,
        out_specs=pl.BlockSpec(memory_space=pltpu.VMEM),
        scratch_shapes=[
            vmem(query_nope.shape, BF16),
            vmem(query_rope.shape, BF16),
            vmem(key_absorb.shape, BF16),
            vmem(value_absorb.shape, BF16),
            vmem((output_weight.shape[0], spaced(output_weight.shape[1])), BF16),
            vmem(latent_cache.shape, BF16),
            dma((8,)),
            vmem(query_nope.shape, F32),
            vmem((requests, heads_here, cut), F32),
            vmem((requests, heads_here, latent - cut), F32),
            vmem((requests, heads, rope), F32),
            vmem((rows, cut), BF16),
            vmem((rows, latent - cut), BF16),
            vmem((ctx, rows, cut), BF16),
            vmem((ctx, rows, latent - cut), BF16),
            vmem((ctx,) + query_rope.shape, BF16),
            dma((gather_sems,)), dma((gather_sems,)), dma((gather_sems,)),
            dma((gather_sems,)), dma((gather_sems,)), dma((gather_sems,)),
            vmem((1, page_count), I32),
            vmem((up_to(GROUP + 4, 8), table_lanes), I32),
            pltpu.SMEM((up_to(GROUP + 4, 8), table_lanes), I32),
            vmem((items, GROUP * page), F32),
            vmem((requests, heads, cut), BF16),
            vmem((requests, heads, latent - cut), BF16),
            vmem((requests, heads, rope), BF16),
            vmem((items, heads, GROUP * page), F32),
            vmem((items, heads, 128), F32),
            vmem((requests, heads, 128), F32),
            vmem((items, heads, latent), F32),
            vmem((2, nz, rows, latent), BF16),
            vmem((2, nz) + stat_tail, F32),
            vmem((nz, rows, latent), BF16),
            vmem((nz,) + stat_tail, F32),
            vmem((nz - 1, rows, latent), BF16),
            vmem((nz - 1,) + stat_tail, F32),
            vmem((nz - 1, rows, latent), BF16),
            vmem((nz - 1,) + stat_tail, F32),
            vmem((requests, heads_here, latent), F32),
            vmem((2 * ctx, requests, half), BF16),
            vmem((2 * ctx, requests, half), BF16),
            dma((nz * PARTS,)), dma((nz * PARTS,)), dma, dma,
            dma(((nz - 1) * PARTS,)), dma(((nz - 1) * PARTS,)), dma((nz - 1,)), dma((nz - 1,)),
            dma((2 * ctx,)), dma((2 * ctx,)),
        ],
        compiler_params=pltpu.CompilerParams(collective_id=0, has_side_effects=True, vmem_limit_bytes=62 << 20),
    )(*operands)


def solution(mesh):
    return jax.shard_map(
        functools.partial(body, mesh.shape["ctx"]),
        mesh=mesh,
        in_specs=(
            P("groups", ("ctx", "head"), None),
            P("groups", ("ctx", "head")),
            P(("ctx", "head"), None, None),
            P(("ctx", "head"), None, None),
            P(("ctx", "head"), None),
            P(("groups", "ctx"), None, None),
            P(("groups", "ctx")),
        ),
        out_specs=P("groups", ("ctx", "head")),
        check_vma=False,
    )
```

```python
import functools

import jax
import jax.numpy as jnp
from jax import lax
from jax.experimental import pallas as pl
from jax.experimental.pallas import tpu as pltpu
from jax.sharding import PartitionSpec as P

PARTS = 2
CUTS = 4
FIRST, SECOND, ROTARY = range(3)
GROUP = 4
BATCH = 3
UNROLLED = 2
F32 = jnp.float32
BF16 = jnp.bfloat16
I32 = jnp.int32
LOW = -1e30


def dot_nt(a, b):
    return lax.dot_general(a, b, (((1,), (1,)), ((), ())), preferred_element_type=F32)


def remote(src, dst, send_sem, recv_sem, where):
    return pltpu.make_async_remote_copy(
        src_ref=src, dst_ref=dst, send_sem=send_sem, recv_sem=recv_sem,
        device_id=where, device_id_type=pl.DeviceIdType.MESH)


def up_to(n, step):
    return -(-n // step) * step


def spaced(columns):
    return (columns // 128 | 1) * 128 if columns % 128 == 0 else columns


def column(row):
    n = row.shape[1]
    diagonal = lax.broadcasted_iota(I32, (n, n), 0) == lax.broadcasted_iota(I32, (n, n), 1)
    return jnp.sum(jnp.where(diagonal, jnp.broadcast_to(row, (n, n)), 0), axis=1, keepdims=True)


def plan_items(owner, requests, group, table, bias):
    count = owner.shape[1]
    width = up_to(count, 128)
    lanes_out = table.shape[1]
    items, tokens = bias.shape
    page = tokens // group
    owner = jnp.where(owner < 0, requests, owner)
    if width > count:
        owner = jnp.concatenate([owner, jnp.full((1, width - count), requests, I32)], axis=1)
    lane = lax.broadcasted_iota(I32, (1, width), 1)
    slot = lax.broadcasted_iota(I32, (width, 1), 0)
    lanes = lax.broadcasted_iota(I32, (width, width), 1)
    places = lax.broadcasted_iota(I32, (width, width), 0)
    key = owner * width + lane
    rank = jnp.sum(jnp.where(jnp.broadcast_to(key, (width, width)) < column(key), 1, 0), axis=1, keepdims=True)
    owner_c = column(owner)
    here = rank == lanes
    order = jnp.sum(jnp.where(here, slot, 0), axis=0, keepdims=True)
    sorted_owner = jnp.sum(jnp.where(here, owner_c, 0), axis=0, keepdims=True)
    sorted_c = column(sorted_owner)
    ahead = jnp.sum(jnp.where(sorted_c < sorted_owner, 1, 0), axis=0, keepdims=True)
    opens = lax.rem(lane - ahead, jnp.full(lane.shape, group, I32)) == 0
    start = column(jnp.where(opens & (sorted_owner < requests), 1, 0))
    order_c = jnp.minimum(column(order), count - 1)
    item = column(jnp.sum(jnp.where(places <= lanes, start, 0), axis=0, keepdims=True) - 1)
    place = lax.broadcasted_iota(I32, (width, lanes_out), 0)
    mine = (item == lax.broadcasted_iota(I32, (width, lanes_out), 1)) & (start > 0)

    def pick(value):
        return jnp.sum(jnp.where(mine, value, 0), axis=0, keepdims=True)

    first, who, real = pick(slot), pick(sorted_c), pick(start)
    tag = jnp.where(real > 0, who, -1)
    tag_c = column(tag)
    table[0:1, :] = who
    for j in range(group):
        chosen = place == first + j
        table[1 + j:2 + j, :] = jnp.sum(jnp.where(chosen, order_c, 0), axis=0, keepdims=True)
        theirs = column(jnp.sum(jnp.where(chosen, sorted_c + 1, 0), axis=0, keepdims=True) - 1)
        fits = jnp.where(theirs[:items] == tag_c[:items], 0.0, LOW)
        bias[:, j * page:(j + 1) * page] = jnp.broadcast_to(fits, (items, page))
    index = lax.broadcasted_iota(I32, (1, lanes_out), 1)
    previous = jnp.where(index == 0, -1, pltpu.roll(tag, 1, 1))
    table[group + 1:group + 2, :] = jnp.where(tag == previous, 1, 0)
    owned = tag_c == lax.broadcasted_iota(I32, (lanes_out, lanes_out), 1)
    number = lax.broadcasted_iota(I32, (lanes_out, lanes_out), 0)
    table[group + 2:group + 3, :] = jnp.max(jnp.where(owned, number, 0), axis=0, keepdims=True)
    table[group + 3:group + 4, :] = jnp.max(jnp.where(owned, 1, 0), axis=0, keepdims=True)


def kernel(ctx, unroll, score_scale, nope_hbm, rope_hbm, key_hbm, owner_hbm, cache_hbm, value_hbm, weight_hbm, out_ref,
           nope_ref, rope_ref, key_ref, value_ref, weight, pages, in_sems, wide, rows_a, rows_b, rows_c, mine_a, mine_b,
           all_a, all_b, all_c, y_send, y_recv, up_send, up_recv, down_send, down_recv,
           owner_ref, table, tab, bias, query_a, query_b, query_c, scores, marks, top_full, acc,
           sums, stats, y_sum, y_stat, c_sum, c_stat, z_sum, z_stat, attended,
           p_out, p_in,
           ys_send, ys_recv, yt_send, yt_recv, zs_send, zs_recv, zt_send, zt_recv,
           p_send, p_recv):
    requests, heads_here, _ = nope_ref.shape
    latent = key_ref.shape[2]
    cut = query_b.shape[2]
    rope = rope_ref.shape[1] // heads_here
    items = scores.shape[0]
    nz = ctx // 2
    half = out_ref.shape[1]
    block = 2 * half
    me, core = lax.axis_index("ctx"), lax.axis_index("head")
    z, y = me // 2, me % 2
    partner, twin = {"ctx": z * 2 + 1 - y}, {"head": 1 - core}
    above, below = {"ctx": me + 2}, {"ctx": me - 2}
    has_above, has_below = z + 1 < nz, z > 0

    def load(i, src, dst):
        return pltpu.make_async_copy(src, dst, in_sems.at[i])

    key_loads = [load(2 + 6 * i, key_hbm.at[:, :, columns], key_ref.at[:, :, columns])
                 for i, columns in enumerate((slice(0, cut), slice(cut, latent)))]
    first_loads = [load(1, rope_hbm, rope_ref), load(0, nope_hbm, nope_ref)] + key_loads
    owner_load = load(3, owner_hbm, owner_ref)
    cache_load, value_load, weight_load = (
        load(4, cache_hbm, pages), load(5, value_hbm, value_ref), load(6, weight_hbm, weight.at[:, :weight_hbm.shape[1]]))
    table_load = load(7, table, tab)
    for copy in first_loads:
        copy.start()
    owner_load.start()

    barrier = pltpu.get_barrier_semaphore()
    for k in range(1, ctx):
        pl.semaphore_signal(barrier, inc=1, device_id={"ctx": (me + k) % ctx}, device_id_type=pl.DeviceIdType.MESH)
        pl.semaphore_signal(barrier, inc=1, device_id={"ctx": (me + k) % ctx, "head": 1 - core},
                            device_id_type=pl.DeviceIdType.MESH)
    pl.semaphore_signal(barrier, inc=1, device_id=twin, device_id_type=pl.DeviceIdType.MESH)

    depth = mine_a.shape[0] // PARTS
    gathered = (all_a, all_b, all_c)

    def lines(part):
        return slice(part * depth, (part + 1) * depth)

    def parts(which):
        return range(1 if which == ROTARY else PARTS)

    def piece(which, part):
        return slice(0, requests) if which == ROTARY else lines(part)

    def block_of(which, row, part):
        return gathered[which].at[row, piece(which, part)]

    def sem(which, step, part):
        return (which * nz + step) * PARTS + part

    def across(which, origin, part, src=None):
        slot, i = block_of(which, origin * 2 + y, part), sem(which, origin, part)
        return remote(slot if src is None else src.at[piece(which, part)], slot, y_send.at[i], y_recv.at[i], partner)

    def upward(which, step, part, src=None):
        slot, i = block_of(which, me - 2 * step, part), sem(which, step, part)
        return remote(slot if src is None else src.at[piece(which, part)], slot, up_send.at[i], up_recv.at[i], above)

    def downward(which, step, part, src=None):
        slot, i = block_of(which, me + 2 * step, part), sem(which, step, part)
        return remote(slot if src is None else src.at[piece(which, part)], slot, down_send.at[i], down_recv.at[i], below)

    def arrival(which, row, part, done):
        slot = block_of(which, row, part)
        return remote(slot, slot, done, done, partner)

    mine = (mine_a, mine_b, rope_ref)

    def send_along(which):
        for part in parts(which):
            @pl.when(has_above)
            def _():
                upward(which, 0, part, mine[which]).start()

            @pl.when(has_below)
            def _():
                downward(which, 0, part, mine[which]).start()

    def send_across(which):
        for part in parts(which):
            across(which, z, part, mine[which]).start()

    first_loads[0].wait()
    pl.semaphore_wait(barrier, 2 * ctx - 1)
    send_along(ROTARY)
    send_across(ROTARY)
    all_c[me] = rope_ref[...]
    first_loads[1].wait()
    wide[...] = nope_ref[...].astype(F32)
    key_loads[0].wait()
    for h in range(heads_here):
        rows_a[:, h, :] = jnp.dot(wide[:, h, :].astype(BF16), key_ref[h, :, :cut], preferred_element_type=F32)
    value = rows_a[...].reshape(requests * heads_here, cut).astype(BF16)
    mine_a[...] = value
    all_a[me] = value
    send_along(FIRST)
    send_across(FIRST)
    key_loads[1].wait()
    cache_load.start()
    for h in range(heads_here):
        rows_b[:, h, :] = jnp.dot(wide[:, h, :].astype(BF16), key_ref[h, :, cut:], preferred_element_type=F32)
    value = rows_b[...].reshape(requests * heads_here, latent - cut).astype(BF16)
    mine_b[...] = value
    all_b[me] = value
    send_along(1)
    send_across(1)
    value_load.start()
    weight_load.start()

    owner_load.wait()
    plan_items(owner_ref[...], requests, GROUP, table, bias)
    table_load.start()

    def pass_on(which, step):
        for part in parts(which):
            @pl.when(z - 1 - step >= 0)
            def _():
                arrival(which, me - 2 * (step + 1), part, up_recv.at[sem(which, step, part)]).wait_recv()
                if step + 1 < nz - 1:
                    @pl.when(has_above)
                    def _():
                        upward(which, step + 1, part).start()
                across(which, z - 1 - step, part).start()

            @pl.when(z + 1 + step < nz)
            def _():
                arrival(which, me + 2 * (step + 1), part, down_recv.at[sem(which, step, part)]).wait_recv()
                if step + 1 < nz - 1:
                    @pl.when(has_below)
                    def _():
                        downward(which, step + 1, part).start()
                across(which, z + 1 + step, part).start()

    for step in range(nz - 1):
        pass_on(2, step)
        pass_on(0, step)
        if 1 <= step < nz - 2:
            pass_on(1, step - 1)

    def settle(which, query):
        for origin in range(nz):
            for part in parts(which):
                arrival(which, origin * 2 + 1 - y, part, y_recv.at[sem(which, origin, part)]).wait_recv()
        if which == ROTARY:
            for c in range(ctx):
                for h in range(heads_here):
                    rows_c[:, c * heads_here + h, :] = all_c[c, :, h * rope:(h + 1) * rope].astype(F32)
            query[...] = rows_c[...].astype(BF16)
            return
        for r in range(requests):
            lots = [gathered[which][c, r * heads_here:(r + 1) * heads_here, :].astype(F32) for c in range(ctx)]
            query[r] = jnp.concatenate(lots, axis=0).astype(BF16)

    table_load.wait()
    cache_load.wait()

    def entries(i, columns):
        return jnp.concatenate([pages[tab[1 + j, i], :, columns] for j in range(GROUP)], axis=0)

    def rope_scores(s, carry):
        for u in range(unroll):
            i = s * unroll + u
            scores[i] = dot_nt(query_c[tab[0, i]], entries(i, slice(latent, latent + rope)))
        return carry

    def first_scores(s, carry):
        for u in range(unroll):
            i = s * unroll + u
            scores[i] = scores[i] + dot_nt(query_a[tab[0, i]], entries(i, slice(0, cut)))
        return carry

    settle(2, query_c)
    slices = items // unroll
    left = [step for step in range(nz - 1) if step == nz - 2 or step == nz - 3]
    for n in range(slices):
        lax.fori_loop(n, n + 1, rope_scores, 0)
        if n < len(left) and n < slices - 1:
            pass_on(1, left[n])
    for step in left[slices - 1:]:
        pass_on(1, step)
    settle(0, query_a)
    lax.fori_loop(0, slices, first_scores, 0)
    settle(1, query_b)

    def last_scores(s, top):
        for u in range(unroll):
            i = s * unroll + u
            found = scores[i] + dot_nt(query_b[tab[0, i]], entries(i, slice(cut, latent)))
            found = found * score_scale + bias[pl.ds(i, 1), :]
            scores[i] = found
            top = jnp.where(tab[GROUP + 1, i] > 0, top, LOW)
            for j in range(found.shape[1] // 128):
                top = jnp.maximum(top, found[:, j * 128:(j + 1) * 128])
            marks[i] = top
        return top

    lax.fori_loop(0, items // unroll, last_scores, jnp.full(marks.shape[1:], LOW, F32))
    for r in range(requests):
        seen = marks[tab[GROUP + 2, r]]
        top_full[r] = jnp.broadcast_to(jnp.max(seen, axis=1, keepdims=True), seen.shape)

    def weigh(s, carry):
        total, held = carry
        for u in range(unroll):
            i = s * unroll + u
            keep = tab[GROUP + 1, i] > 0
            top = top_full[tab[0, i]]
            total = jnp.where(keep, total, 0.0)
            weights = []
            for j in range(scores.shape[2] // 128):
                weight_j = jnp.exp(scores[i, :, j * 128:(j + 1) * 128] - top)
                total = total + weight_j
                weights.append(weight_j.astype(BF16))
            marks[i] = total
            held = jnp.where(keep, held, 0.0) + jnp.dot(
                jnp.concatenate(weights, axis=1), entries(i, slice(0, latent)), preferred_element_type=F32)
            acc[i] = held
        return total, held

    lax.fori_loop(0, items // unroll, weigh, (jnp.zeros(marks.shape[1:], F32), jnp.zeros(acc.shape[1:], F32)))

    lane = lax.broadcasted_iota(I32, marks.shape[1:], 1)
    top = jnp.full(lane.shape, LOW, F32)
    norm = jnp.zeros(lane.shape, F32)
    for r in range(requests):
        here = (lane == r) & jnp.broadcast_to(tab[GROUP + 3, r] > 0, lane.shape)
        top = jnp.where(here, top_full[r], top)
        norm = jnp.where(here, jnp.sum(marks[tab[GROUP + 2, r]], axis=1, keepdims=True), norm)
    for c in range(ctx):
        rows = slice(c * heads_here, (c + 1) * heads_here)
        stats[c % 2, c // 2, 0] = top[rows]
        stats[c % 2, c // 2, 1] = norm[rows]
        lots = [acc[tab[GROUP + 2, r], rows, :] for r in range(requests)]
        sums[c % 2, c // 2] = jnp.concatenate(lots, axis=0).astype(BF16)

    def opposite(k):
        return z ^ (nz - 1 - k) if nz & (nz - 1) == 0 else (z + 1 + k) % nz

    thin = y_sum.shape[1] // CUTS

    def rows_of(part):
        return slice(part * thin, (part + 1) * thin)

    stat_copy = remote(stats.at[1 - y], y_stat, yt_send, yt_recv, partner)
    stat_copy.start()
    y_copies = []
    for k in range(nz):
        target = opposite(k)
        for part in range(CUTS):
            i = k * CUTS + part
            copy = remote(sums.at[1 - y, target, rows_of(part)], y_sum.at[k, rows_of(part)],
                          ys_send.at[i], ys_recv.at[i], partner)
            copy.start()
            y_copies.append(copy)
    stat_copy.wait_recv()

    def spread(factor):
        return jnp.concatenate([factor[:, r:r + 1] for r in range(requests)], axis=0)

    z_copies, z_stats = [], []
    for k in range(nz):
        target = opposite(k)
        top_a, norm_a = stats[y, target, 0], stats[y, target, 1]
        top_b, norm_b = y_stat[target, 0], y_stat[target, 1]
        top = jnp.maximum(top_a, top_b)
        keep_a, keep_b = jnp.exp(top_a - top), jnp.exp(top_b - top)
        norm = keep_a * norm_a + keep_b * norm_b
        rows_x, rows_y = spread(keep_a), spread(keep_b)
        there = {"ctx": target * 2 + y}
        if k < nz - 1:
            c_stat[k, 0] = top
            c_stat[k, 1] = norm
            copy = remote(c_stat.at[k], z_stat.at[k], zt_send.at[k], zt_recv.at[k], there)
            copy.start()
            z_stats.append(copy)
        both = []
        for part in range(CUTS):
            i = k * CUTS + part
            y_copies[i].wait_recv()
            both.append(rows_x[rows_of(part)] * sums[y, target, rows_of(part)].astype(F32)
                        + rows_y[rows_of(part)] * y_sum[k, rows_of(part)].astype(F32))
            if k < nz - 1:
                c_sum[k, rows_of(part)] = both[part].astype(BF16)
                copy = remote(c_sum.at[k, rows_of(part)], z_sum.at[k, rows_of(part)], zs_send.at[i], zs_recv.at[i], there)
                copy.start()
                z_copies.append(copy)
    both = jnp.concatenate(both, axis=0)
    for copy in z_stats:
        copy.wait_recv()
    highest = top
    for k in range(nz - 1):
        highest = jnp.maximum(highest, z_stat[k, 0])
    keep = jnp.exp(top - highest)
    all_norm = keep * norm
    factors = []
    for k in range(nz - 1):
        factors.append(jnp.exp(z_stat[k, 0] - highest))
        all_norm = all_norm + factors[k] * z_stat[k, 1]
    safe = jnp.where(all_norm > 0, all_norm, 1.0)
    total = spread(keep / safe) * both
    for k in range(nz - 1):
        for part in range(CUTS):
            z_copies[k * CUTS + part].wait_recv()
        total = total + spread(factors[k] / safe) * z_sum[k].astype(F32)
    attended[...] = total.reshape(requests, heads_here, latent)
    outs = []
    value_load.wait()
    for h in range(heads_here):
        outs.append(jnp.dot(attended[:, h, :].astype(BF16), value_ref[h], preferred_element_type=F32).astype(BF16))
    head_out = jnp.concatenate(outs, axis=1)
    weight_load.wait()

    aligned = block % 128 == 0
    powers = ctx & (ctx - 1) == 0
    own = ctx - 1 if aligned else 0

    def place(k):
        if not aligned:
            return k
        return me ^ (ctx - 1 - k) if powers else (me + 1 + k) % ctx

    def send_out(k, side):
        target = place(k)
        slot = (k if aligned else (target - me + ctx) % ctx) * 2 + core
        return remote(p_out.at[k * 2 + side], p_in.at[slot], p_send.at[k * 2 + side], p_recv.at[slot],
                      {"ctx": target, "head": side})

    def each_out(k, act):
        for side in range(2):
            if aligned and k != own:
                act(send_out(k, side))
            else:
                @pl.when((place(k) != me) | (core != side))
                def _():
                    act(send_out(k, side))

    for base in range(0, ctx, BATCH):
        batch = range(base, min(base + BATCH, ctx))
        for k in batch:
            if aligned:
                columns = weight[:, pl.ds(pl.multiple_of(place(k) * block, 128), block)]
            else:
                columns = weight[:, k * block:(k + 1) * block]
            part = jnp.dot(head_out, columns, preferred_element_type=F32).astype(BF16)
            p_out[k * 2] = part[:, :half]
            p_out[k * 2 + 1] = part[:, half:]
        for k in batch:
            each_out(k, lambda copy: copy.start())
    result = p_out[(own if aligned else me) * 2 + core].astype(F32)
    for k in range(ctx):
        for side in range(2):
            slot = k * 2 + side
            if k != own:
                remote(p_in.at[slot], p_in.at[slot], p_recv.at[slot], p_recv.at[slot], twin).wait_recv()
                result = result + p_in[slot].astype(F32)
    far = own * 2 + 1 - core
    remote(p_in.at[far], p_in.at[far], p_recv.at[far], p_recv.at[far], twin).wait_recv()
    result = result + p_in[far].astype(F32)
    out_ref[...] = result.astype(BF16)
    for k in range(ctx):
        each_out(k, lambda copy: copy.wait_send())
    for copy in z_copies + z_stats + y_copies + [stat_copy]:
        copy.wait_send()
    for which in (FIRST, SECOND, ROTARY):
        for part in parts(which):
            for origin in range(nz):
                across(which, origin, part, mine[which]).wait_send()
            for step in range(nz - 1):
                @pl.when(has_above & (z - step >= 0))
                def _():
                    upward(which, step, part, mine[which]).wait_send()

                @pl.when(has_below & (z + step < nz))
                def _():
                    downward(which, step, part, mine[which]).wait_send()


def body(ctx, query_nope, query_rope, key_absorb, value_absorb, output_weight, latent_cache, page_owner):
    requests, heads_here, nope = query_nope.shape
    latent = key_absorb.shape[2]
    rope = query_rope.shape[1] // heads_here
    page_count, page, entry = latent_cache.shape
    heads = ctx * heads_here
    cut = latent // 2
    rows = requests * heads_here
    nz = ctx // 2
    half = output_weight.shape[1] // (2 * ctx)
    wanted = (page_count + (GROUP - 1) * requests) // GROUP
    unroll = -(-wanted // UNROLLED)
    items = up_to(wanted, unroll)
    table_lanes = up_to(items, 128)
    vmem, dma = pltpu.VMEM, pltpu.SemaphoreType.DMA
    gather_sems = 3 * nz * PARTS
    stat_tail = (2, heads_here, 128)
    operands = [query_nope, query_rope, key_absorb, page_owner.reshape(1, page_count), latent_cache, value_absorb,
                output_weight]
    operands = [pltpu.with_memory_space_constraint(x, pltpu.HBM) for x in operands]
    return pl.pallas_call(
        functools.partial(kernel, ctx, unroll, (nope + rope) ** (-0.5)),
        out_shape=pltpu.VMEM((requests, half), BF16),
        in_specs=[pl.BlockSpec(memory_space=pltpu.HBM)] * 7,
        out_specs=pl.BlockSpec(memory_space=pltpu.VMEM),
        scratch_shapes=[
            vmem(query_nope.shape, BF16),
            vmem(query_rope.shape, BF16),
            vmem(key_absorb.shape, BF16),
            vmem(value_absorb.shape, BF16),
            vmem((output_weight.shape[0], spaced(output_weight.shape[1])), BF16),
            vmem(latent_cache.shape, BF16),
            dma((9,)),
            vmem(query_nope.shape, F32),
            vmem((requests, heads_here, cut), F32),
            vmem((requests, heads_here, latent - cut), F32),
            vmem((requests, heads, rope), F32),
            vmem((rows, cut), BF16),
            vmem((rows, latent - cut), BF16),
            vmem((ctx, rows, cut), BF16),
            vmem((ctx, rows, latent - cut), BF16),
            vmem((ctx,) + query_rope.shape, BF16),
            dma((gather_sems,)), dma((gather_sems,)), dma((gather_sems,)),
            dma((gather_sems,)), dma((gather_sems,)), dma((gather_sems,)),
            vmem((1, page_count), I32),
            vmem((up_to(GROUP + 4, 8), table_lanes), I32),
            pltpu.SMEM((up_to(GROUP + 4, 8), table_lanes), I32),
            vmem((items, GROUP * page), F32),
            vmem((requests, heads, cut), BF16),
            vmem((requests, heads, latent - cut), BF16),
            vmem((requests, heads, rope), BF16),
            vmem((items, heads, GROUP * page), F32),
            vmem((items, heads, 128), F32),
            vmem((requests, heads, 128), F32),
            vmem((items, heads, latent), F32),
            vmem((2, nz, rows, latent), BF16),
            vmem((2, nz) + stat_tail, F32),
            vmem((nz, rows, latent), BF16),
            vmem((nz,) + stat_tail, F32),
            vmem((nz - 1, rows, latent), BF16),
            vmem((nz - 1,) + stat_tail, F32),
            vmem((nz - 1, rows, latent), BF16),
            vmem((nz - 1,) + stat_tail, F32),
            vmem((requests, heads_here, latent), F32),
            vmem((2 * ctx, requests, half), BF16),
            vmem((2 * ctx, requests, half), BF16),
            dma((nz * CUTS,)), dma((nz * CUTS,)), dma, dma,
            dma(((nz - 1) * CUTS,)), dma(((nz - 1) * CUTS,)), dma((nz - 1,)), dma((nz - 1,)),
            dma((2 * ctx,)), dma((2 * ctx,)),
        ],
        compiler_params=pltpu.CompilerParams(collective_id=0, has_side_effects=True, vmem_limit_bytes=58 << 20),
    )(*operands)


def solution(mesh):
    return jax.shard_map(
        functools.partial(body, mesh.shape["ctx"]),
        mesh=mesh,
        in_specs=(
            P("groups", ("ctx", "head"), None),
            P("groups", ("ctx", "head")),
            P(("ctx", "head"), None, None),
            P(("ctx", "head"), None, None),
            P(("ctx", "head"), None),
            P(("groups", "ctx"), None, None),
            P(("groups", "ctx")),
        ),
        out_specs=P("groups", ("ctx", "head")),
        check_vma=False,
    )
```
